256 devices in a mesh: head: 8 (over y, core), inner: 16 (over x_lo, z), outer: 2 (over x_hi).
Axes of the slice: x: 4 (x_hi: 2, x_lo: 2; x = x_hi * 2 + x_lo), y: 4, z: 8, core: 2. Of those that a mesh axis runs over, the one named last changes fastest.
Arguments:
- queries: bfloat16 [16384, 8192], P(('inner', 'outer', 'head')), may hold values from -12.816310409006173 to 12.816310409006173
- keys: bfloat16 [16384, 1024], P(('inner', 'outer', 'head')), may hold values from -4 to 4
- values: bfloat16 [16384, 1024], P(('inner', 'outer', 'head')), may hold values from -6 to 6
- dout: bfloat16 [16384, 8192], P(('inner', 'outer', 'head')), may hold values from -6 to 6
- doc_lengths: int32 [128], replicated, may hold values from 1 to 256, 16384 in all
- span_order: int32 [64], replicated, may hold values from 0 to 63, as said below
Outputs:
- attended: bfloat16 [16384, 8192], P(('inner', 'outer', 'head'))
- entropy: float32 [16384, 64], P(('inner', 'outer'), 'head')
- grad_query: bfloat16 [16384, 8192], P(('inner', 'outer', 'head'))
- grad_key: bfloat16 [16384, 1024], P(('inner', 'outer', 'head'))
- grad_value: bfloat16 [16384, 1024], P(('inner', 'outer', 'head'))
The draws below stay inside these ranges and needn't reach their ends.
Inputs may be any that keep to these rules, and one draw needn't show every extreme that they name: `doc_lengths`: the 128 documents lie one after another over the 16384 positions of the sequence; the lengths sum to 16384 and the longest is exactly 256. Stored rows b * 256 to (b + 1) * 256 - 1 hold the sequence positions span_order[b] * 256 onward, in order; stored blocks 2 i and 2 i + 1 hold the spans i and 63 - i, in either order.
All inputs are finite; a program needn't handle non-finite values.
Results may differ from the reference program's by a relative error of at most 0.03.
Values may be sent and summed in bfloat16 or wider, within the bound.
A program may use at most 64 MiB of HBM per device.

```python
import math
import jax
import jax.numpy as jnp
import numpy as np
from jax import lax

QUERY_HEADS = 64
KEY_VALUE_HEADS = 8
HEAD_WIDTH = 128
SPAN_TOKENS = 256
NCHUNK = 64
SEQUENCE_TOKENS = 16384
DOC_MAX = 256
NDOC = 128


def draw_keys(key, part):
    sampled_values = jnp.clip(jax.random.normal(jax.random.fold_in(key, 11), (SEQUENCE_TOKENS, KEY_VALUE_HEADS * HEAD_WIDTH), jnp.float32), -4.0, 4.0)
    return sampled_values.astype(jnp.bfloat16)


def draw_queries(key, part):
    sampled_values = jnp.clip(jax.random.normal(jax.random.fold_in(key, 12), (SEQUENCE_TOKENS, QUERY_HEADS * HEAD_WIDTH), jnp.float32), -4.0, 4.0)
    return sampled_values.astype(jnp.bfloat16)


def draw_span_order(key, part):
    half_count = NCHUNK // 2
    swaps = jax.random.randint(jax.random.fold_in(key, 21), (half_count,), 0, 2)
    device_ids = jnp.arange(half_count, dtype=jnp.int32)
    lower_ids = device_ids
    upper_ids = NCHUNK - 1 - device_ids
    first_ids = jnp.where(swaps == 0, lower_ids, upper_ids)
    second_ids = jnp.where(swaps == 0, upper_ids, lower_ids)
    return jnp.stack([first_ids, second_ids], axis=1).reshape(NCHUNK).astype(jnp.int32)


def block_scale(stream_key, shape, shards, smallest, high):
    def one(dim, blocks):
        draws = jax.random.uniform(jax.random.fold_in(jax.random.fold_in(stream_key, 6), dim), (blocks,), jnp.float32, smallest / len(shards), high / len(shards))
        return jnp.repeat(jnp.exp(draws), shape[dim] // blocks).reshape((-1,) + (1,) * (len(shape) - dim - 1))

    factor_of = one(*shards[0])
    for cut in shards[1:]:
        factor_of = factor_of * one(*cut)
    return factor_of


def profile(count, total, most, skew):
    portions = [(1 << 20) // math.isqrt(standing ** skew) + 1 for standing in range(2, count + 1)]
    spare, given = total - most - (count - 1), [1] * (count - 1)
    while spare > 0:
        movable = [i for i in range(count - 1) if given[i] < most]
        whole, budget = sum([portions[i] for i in movable]), spare
        for i in movable:
            more = min(most - given[i], max(1, budget * portions[i] // whole), spare)
            given[i] = given[i] + more
            spare = spare - more
    return np.array([most] + given)


def uneven_parts(own_key, amount, total, limit, lean):
    if amount == 2:
        one = jax.random.randint(own_key, (), max(1, total - limit), min(limit, total - 1) + 1)
        return jnp.stack([one, total - one])
    tallies = jnp.asarray(profile(amount, total, limit, lean), jnp.int32)
    twos = (amount - 1) // 2
    donor, taker = tallies[1:1 + 2 * twos:2], tallies[2:2 + 2 * twos:2]
    room = jnp.minimum(donor - 1, limit - taker)
    shifted = jax.random.randint(jax.random.fold_in(own_key, 1), (twos,), 0, 1 << 20) % (room + 1)
    tallies = tallies.at[1:1 + 2 * twos:2].set(donor - shifted).at[2:2 + 2 * twos:2].set(taker + shifted)
    return tallies[jax.random.permutation(jax.random.fold_in(own_key, 2), amount)]


def scatter_about(key, dims, width, reach, cuts=(), kind=jnp.bfloat16):
    drawn = jax.random.normal(key, dims, jnp.float32) * width
    if len(cuts) > 0:
        drawn = block_scale(key, dims, cuts, -0.22, 0.18) * drawn
    return jnp.clip(drawn, min=-reach, max=reach).astype(kind)


def setup_inputs(seed: int = 0) -> dict:
    key_list = jax.random.split(jax.random.key(seed), 7)
    queries = draw_queries(jax.random.fold_in(key_list[6], 71), 0)
    keys = draw_keys(jax.random.fold_in(key_list[6], 71), 0)
    values = scatter_about(key_list[2], (SEQUENCE_TOKENS, KEY_VALUE_HEADS * HEAD_WIDTH), 1.0, 6.0, ((0, 256),))
    dout = scatter_about(key_list[3], (SEQUENCE_TOKENS, QUERY_HEADS * HEAD_WIDTH), 1.0, 6.0, ((0, 256),))
    doc_lengths = uneven_parts(key_list[4], NDOC, SEQUENCE_TOKENS, DOC_MAX, 2).astype(jnp.int32)
    span_order = draw_span_order(jax.random.fold_in(key_list[6], 71), 0)
    return dict(queries=queries, keys=keys, values=values, dout=dout, doc_lengths=doc_lengths, span_order=span_order)


def doc_index(positions, doc_lengths):
    starts = jnp.cumsum(doc_lengths) - doc_lengths
    return lax.optimization_barrier(jnp.sum((starts[None, :] <= positions[:, None]).astype(jnp.int32), axis=1)) - 1

def reference(queries, keys, values, dout, doc_lengths, span_order):
    heads_per_group = QUERY_HEADS // KEY_VALUE_HEADS
    doc_reach = (DOC_MAX - 1) // SPAN_TOKENS + 1
    tolerance_gap = doc_reach * SPAN_TOKENS
    visible_window = tolerance_gap + SPAN_TOKENS
    blocks = jnp.arange(NCHUNK, dtype=jnp.int32)
    inverse = jnp.zeros((NCHUNK,), jnp.int32).at[span_order].set(blocks)

    def to_sequence(source):
        return source.reshape(NCHUNK, SPAN_TOKENS, source.shape[1])[inverse].reshape(SEQUENCE_TOKENS, source.shape[1])

    def to_stored(source):
        return source.reshape(NCHUNK, SPAN_TOKENS, source.shape[1])[span_order].reshape(SEQUENCE_TOKENS, source.shape[1])
    sequence_queries = to_sequence(queries)
    sequence_keys = jnp.pad(to_sequence(keys), ((tolerance_gap, 0), (0, 0)))
    sequence_values = jnp.pad(to_sequence(values), ((tolerance_gap, 0), (0, 0)))
    sequence_output_gradient = to_sequence(dout)
    positions = jnp.arange(SEQUENCE_TOKENS + tolerance_gap, dtype=jnp.int32) - tolerance_gap
    documents = jnp.where(positions >= 0, doc_index(positions, doc_lengths), -1)

    def one_span(state_now, span_index):
        grad_keys, grad_values = state_now
        leading_row = (span_index * SPAN_TOKENS).astype(jnp.int32)
        query_matrix_rows = lax.dynamic_slice_in_dim(sequence_queries, leading_row, SPAN_TOKENS, 0).astype(jnp.float32).reshape(SPAN_TOKENS, KEY_VALUE_HEADS, heads_per_group, HEAD_WIDTH)
        output_gradient_rows = lax.dynamic_slice_in_dim(sequence_output_gradient, leading_row, SPAN_TOKENS, 0).astype(jnp.float32).reshape(SPAN_TOKENS, KEY_VALUE_HEADS, heads_per_group, HEAD_WIDTH)
        key_matrix_rows = lax.dynamic_slice_in_dim(sequence_keys, leading_row, visible_window, 0).astype(jnp.float32).reshape(visible_window, KEY_VALUE_HEADS, HEAD_WIDTH)
        value_matrix_rows = lax.dynamic_slice_in_dim(sequence_values, leading_row, visible_window, 0).astype(jnp.float32).reshape(visible_window, KEY_VALUE_HEADS, HEAD_WIDTH)
        q_pos = lax.dynamic_slice_in_dim(positions, leading_row + tolerance_gap, SPAN_TOKENS, 0)
        q_doc = lax.dynamic_slice_in_dim(documents, leading_row + tolerance_gap, SPAN_TOKENS, 0)
        k_pos = lax.dynamic_slice_in_dim(positions, leading_row, visible_window, 0)
        k_doc = lax.dynamic_slice_in_dim(documents, leading_row, visible_window, 0)
        allowed = (q_doc[:, None] == k_doc[None, :]) & (k_pos[None, :] <= q_pos[:, None])
        scores = jnp.einsum('qhgd,thd->hgqt', query_matrix_rows, key_matrix_rows) / math.sqrt(HEAD_WIDTH)
        scores = jnp.where(allowed, scores, -jnp.inf)
        row_top = lax.optimization_barrier(jnp.max(scores, axis=-1))
        lse = row_top + jnp.log(lax.optimization_barrier(jnp.sum(jnp.exp(scores - row_top[..., None]), axis=-1)))
        probs = jnp.exp(scores - lse[..., None])
        rounded_result = lax.optimization_barrier(probs.astype(jnp.bfloat16)).astype(jnp.float32)
        out_rows = jnp.einsum('hgqt,thd->qhgd', rounded_result, value_matrix_rows).astype(jnp.bfloat16)
        entropy = lse - lax.optimization_barrier(jnp.sum(jnp.where(allowed, probs * scores, 0.0), axis=-1))
        delta = jnp.transpose(lax.optimization_barrier(jnp.sum(output_gradient_rows * out_rows.astype(jnp.float32), axis=-1)), (1, 2, 0))
        dprobs = jnp.einsum('qhgd,thd->hgqt', output_gradient_rows, value_matrix_rows)
        score_gradient = probs * (dprobs - delta[..., None]) / math.sqrt(HEAD_WIDTH)
        score_gradient = lax.optimization_barrier(score_gradient.astype(jnp.bfloat16)).astype(jnp.float32)
        dquery = jnp.einsum('hgqt,thd->qhgd', score_gradient, key_matrix_rows).astype(jnp.bfloat16)
        key_gradient = jnp.einsum('ysfj,fysm->jym', score_gradient, query_matrix_rows).reshape(visible_window, KEY_VALUE_HEADS * HEAD_WIDTH)
        value_gradient = jnp.einsum('ysfj,fysm->jym', rounded_result, output_gradient_rows).reshape(visible_window, KEY_VALUE_HEADS * HEAD_WIDTH)
        grad_keys = lax.dynamic_update_slice_in_dim(grad_keys, lax.dynamic_slice_in_dim(grad_keys, leading_row, visible_window, 0) + key_gradient, leading_row, 0)
        grad_values = lax.dynamic_update_slice_in_dim(grad_values, lax.dynamic_slice_in_dim(grad_values, leading_row, visible_window, 0) + value_gradient, leading_row, 0)
        produced = (out_rows.reshape(SPAN_TOKENS, QUERY_HEADS * HEAD_WIDTH), jnp.transpose(entropy, (2, 0, 1)).reshape(SPAN_TOKENS, QUERY_HEADS), dquery.reshape(SPAN_TOKENS, QUERY_HEADS * HEAD_WIDTH))
        return ((grad_keys, grad_values), produced)
    blank_gradients = jnp.zeros((SEQUENCE_TOKENS + tolerance_gap, KEY_VALUE_HEADS * HEAD_WIDTH), jnp.float32)
    (grad_keys, grad_values), (outs, entropies, dqueries) = lax.scan(one_span, (blank_gradients, blank_gradients), blocks)
    attended = to_stored(outs.reshape(SEQUENCE_TOKENS, QUERY_HEADS * HEAD_WIDTH))
    entropy = to_stored(entropies.reshape(SEQUENCE_TOKENS, QUERY_HEADS))
    grad_query = to_stored(dqueries.reshape(SEQUENCE_TOKENS, QUERY_HEADS * HEAD_WIDTH))
    grad_key = to_stored(grad_keys[tolerance_gap:].astype(jnp.bfloat16))
    grad_value = to_stored(grad_values[tolerance_gap:].astype(jnp.bfloat16))
    return (attended, entropy, grad_query, grad_key, grad_value)
```

```python
import functools
import math

import jax
import jax.numpy as jnp
from jax import lax
from jax.experimental import pallas as pl
from jax.experimental.pallas import tpu as pltpu
from jax.sharding import PartitionSpec as P

MESH = pl.DeviceIdType.MESH
F32 = jnp.float32
BF16 = jnp.bfloat16
NEG = -1.0e30
LN2 = math.log(2.0)

D = 128
HEADS = 8
ROWS = 64
SPAN = 256
KEYS = 320
STEPS = SPAN // ROWS


def place():
    me = lax.axis_index("head")
    outer_size = lax.axis_size("outer")
    cycle = lax.axis_size("inner") * outer_size
    own = lax.axis_index("inner") * outer_size + lax.axis_index("outer")

    def at(index):
        return {"inner": index // outer_size, "outer": lax.rem(index, outer_size)}

    above = at(lax.rem(own + 1, cycle))
    below = at(lax.rem(own + cycle - 1, cycle))
    return me, me // STEPS, lax.rem(me, STEPS), own, cycle, above, below


def greet(me, above, below):
    barrier = pltpu.get_barrier_semaphore()
    for step in range(1, HEADS):
        pl.semaphore_signal(
            barrier, inc=1, device_id={"head": lax.rem(me + step, HEADS)}, device_id_type=MESH
        )
    pl.semaphore_signal(barrier, inc=1, device_id=above, device_id_type=MESH)
    pl.semaphore_signal(barrier, inc=1, device_id=below, device_id_type=MESH)
    pl.semaphore_wait(barrier, HEADS + 1)


def remote(src, dst, send, recv, device):
    return pltpu.make_async_remote_copy(
        src_ref=src, dst_ref=dst, send_sem=send, recv_sem=recv, device_id=device, device_id_type=MESH
    )


def gather_kernel(
    order_ref, k_ref, v_ref, kk_ref, vv_ref,
    hb, nb, rb, sel,
    s1_send, s1_recv, own_send, own_recv, s2_send, s2_recv, s3_send, s3_recv, local,
):
    me, half, j, own, cycle, above, below = place()
    ins, outs = (k_ref, v_ref), (kk_ref, vv_ref)
    first_low = order_ref[2 * own] == own
    greet(me, above, below)

    def spread(p, kv, src):
        return remote(
            ins[kv].at[:, pl.ds(p * D, D)], hb.at[kv, pl.ds(src * ROWS, ROWS)],
            s1_send.at[p, kv], s1_recv.at[src, kv], {"head": p},
        )

    for p in range(HEADS):
        @pl.when(me != p)
        def _(p=p):
            for kv in range(2):
                spread(p, kv, me).start()

    own_rows = pl.ds(SPAN + j * ROWS, ROWS)
    mine = [
        pltpu.make_async_copy(
            ins[kv].at[:, pl.ds(me * D, D)], hb.at[kv, pl.ds(me * ROWS, ROWS)], local.at[kv]
        )
        for kv in range(2)
    ] + [
        pltpu.make_async_copy(ins[kv], outs[kv].at[own_rows], local.at[2 + kv]) for kv in range(2)
    ]
    for copy in mine:
        copy.start()
    for copy in mine:
        copy.wait()
    for p in range(HEADS):
        @pl.when(me != p)
        def _(p=p):
            for kv in range(2):
                spread(p, kv, p).wait_recv()

    a, b = hb[:, :SPAN], hb[:, SPAN:]
    nb[0] = jnp.where(first_low, a, b)
    nb[1] = jnp.where(first_low, b, a)
    low = remote(nb.at[0], rb.at[0], s2_send.at[0], s2_recv.at[0], above)
    high = remote(nb.at[1], rb.at[1], s2_send.at[1], s2_recv.at[1], below)
    low.start()
    high.start()

    def share(jj, kv, src):
        return remote(
            ins[kv], outs[kv].at[pl.ds(SPAN + src * ROWS, ROWS)],
            own_send.at[jj, kv], own_recv.at[src, kv], {"head": half * STEPS + jj},
        )

    for jj in range(1, STEPS):
        @pl.when(j < jj)
        def _(jj=jj):
            for kv in range(2):
                share(jj, kv, j).start()

    low.wait_recv()
    high.wait_recv()
    prev_low = rb[0]
    prev_high = jnp.where(own == cycle - 1, nb[0], rb[1])
    sel[0] = jnp.where(first_low, prev_low, prev_high)
    sel[1] = jnp.where(first_low, prev_high, prev_low)

    def deliver(p, kv, src, jj):
        rows = pl.ds(jj * ROWS, SPAN - jj * ROWS)
        return remote(
            sel.at[p // STEPS, kv, rows], outs[kv].at[rows, pl.ds(src * D, D)],
            s3_send.at[p, kv], s3_recv.at[src, kv], {"head": p},
        )

    for p in range(HEADS):
        @pl.when(me != p)
        def _(p=p):
            for kv in range(2):
                deliver(p, kv, me, p % STEPS).start()

    back = [
        pltpu.make_async_copy(
            sel.at[half, kv], outs[kv].at[pl.ds(0, SPAN), pl.ds(me * D, D)], local.at[kv]
        )
        for kv in range(2)
    ]
    for copy in back:
        copy.start()
    for jj in range(STEPS):
        @pl.when(j == jj)
        def _(jj=jj):
            for p in range(HEADS):
                @pl.when(me != p)
                def _(p=p):
                    for kv in range(2):
                        deliver(p, kv, p, jj).wait_recv()
    for jj in range(STEPS - 1):
        @pl.when(jj < j)
        def _(jj=jj):
            for kv in range(2):
                share(0, kv, jj).wait_recv()
    for copy in back:
        copy.wait()
    for p in range(HEADS):
        @pl.when(me != p)
        def _(p=p):
            for kv in range(2):
                spread(p, kv, me).wait_send()
                deliver(p, kv, me, p % STEPS).wait_send()
    for jj in range(1, STEPS):
        @pl.when(j < jj)
        def _(jj=jj):
            for kv in range(2):
                share(jj, kv, j).wait_send()
    low.wait_send()
    high.wait_send()


def attend_kernel(
    order_ref, len_ref, q_ref, do_ref, k_ref, v_ref,
    out_ref, dq_ref, gk_ref, gv_ref, ok_ref, ov_ref, ent_ref,
    bias_ref,
):
    me, half, j, own, cycle, above, below = place()
    rows = pl.multiple_of(j * ROWS, ROWS)

    @pl.when(pl.program_id(0) == 0)
    def _():
        start_pos = order_ref[2 * own + half] * SPAN + j * ROWS
        lens = jnp.broadcast_to(len_ref[...], (D, D)).astype(F32)
        row = lax.broadcasted_iota(jnp.int32, (D, D), 0)
        col = lax.broadcasted_iota(jnp.int32, (D, D), 1)
        starts = jnp.sum(jnp.where(col < row, lens, 0.0), axis=1, keepdims=True)
        lane = lax.broadcasted_iota(jnp.int32, (D, D), 1) % ROWS
        pos = (start_pos + lane).astype(F32)
        found = jnp.max(jnp.where(starts <= pos, starts, 0.0), axis=0, keepdims=True)
        first = found.astype(jnp.int32) - (start_pos - SPAN)
        key = lax.broadcasted_iota(jnp.int32, (KEYS, D), 0)
        query = lax.broadcasted_iota(jnp.int32, (KEYS, D), 1) % ROWS
        allowed = (key >= first) & (key <= query + SPAN)
        bias_ref[...] = jnp.where(allowed, 0.0, NEG)

    k5 = k_ref[pl.ds(rows, KEYS), :]
    v5 = v_ref[pl.ds(rows, KEYS), :]
    k5t, v5t = k5.T, v5.T
    scale = 1.0 / math.sqrt(D)
    nt = (((1,), (1,)), ((), ()))
    nn = (((1,), (0,)), ((), ()))
    per = 4
    lanes = per * ROWS
    bias = jnp.concatenate([bias_ref[...]] * (lanes // D), axis=1)
    sub = lax.broadcasted_iota(jnp.int32, (HEADS, D), 0)
    ent = jnp.zeros((HEADS, D), F32)
    dk = jnp.zeros((KEYS, D), F32)
    dv = jnp.zeros((KEYS, D), F32)
    for chunk in range(HEADS // per):
        heads = range(chunk * per, (chunk + 1) * per)
        q = jnp.concatenate([q_ref[:, g * D : (g + 1) * D] for g in heads], axis=0)
        do = jnp.concatenate([do_ref[:, g * D : (g + 1) * D] for g in heads], axis=0)
        t = lax.dot_general(k5, q, nt, preferred_element_type=F32) * (scale / LN2) + bias
        dp = lax.dot_general(v5, do, nt, preferred_element_type=F32)
        u = t - jnp.max(t, axis=0, keepdims=True)
        e = jnp.exp2(u)
        total = jnp.sum(e, axis=0, keepdims=True)
        inv = 1.0 / total
        p = e * inv
        spread = jnp.sum(p * u, axis=0, keepdims=True)
        entropy = LN2 * (jnp.log2(total) - spread)
        pb = p.astype(BF16)
        delta = jnp.sum(p * dp, axis=0, keepdims=True)
        ds = (p * ((dp - delta) * scale)).astype(BF16)
        out = lax.dot_general(v5t, pb, nn, preferred_element_type=F32)
        dq = lax.dot_general(k5t, ds, nn, preferred_element_type=F32)
        dv = dv + lax.dot_general(pb, do, nn, preferred_element_type=F32)
        dk = dk + lax.dot_general(ds, q, nn, preferred_element_type=F32)
        out_t, dq_t = out.T.astype(BF16), dq.T.astype(BF16)
        for n, g in enumerate(heads):
            out_ref[:, g * D : (g + 1) * D] = out_t[n * ROWS : (n + 1) * ROWS]
            dq_ref[:, g * D : (g + 1) * D] = dq_t[n * ROWS : (n + 1) * ROWS]
        for n in range(per // 2):
            pair = jnp.broadcast_to(entropy[:, n * D : (n + 1) * D], (HEADS, D))
            g = chunk * per + 2 * n
            ent = jnp.where(sub == g, pair, ent)
            ent = jnp.where(sub == g + 1, pltpu.roll(pair, ROWS, 1), ent)
    ent_ref[0] = ent
    gk_ref[pl.ds(rows, SPAN), :] = dk[:SPAN].astype(BF16)
    gv_ref[pl.ds(rows, SPAN), :] = dv[:SPAN].astype(BF16)
    ok_ref[...] = dk[SPAN:]
    ov_ref[...] = dv[SPAN:]


def scatter_kernel(
    order_ref, gk_ref, gv_ref, ok_ref, ov_ref, ent_ref, dk_ref, dv_ref, ent_out,
    cb, nb, rb, sb, xb, ob, eb,
    s3_send, s3_recv, own_send, own_recv, s2_send, s2_recv, s1_send, s1_recv, e_send, e_recv, local,
):
    me, half, j, own, cycle, above, below = place()
    grads, owns, outs = (gk_ref, gv_ref), (ok_ref, ov_ref), (dk_ref, dv_ref)
    first_low = order_ref[2 * own] == own
    greet(me, above, below)

    def collect(p, kv, src, jj):
        rows = pl.ds(jj * ROWS, SPAN - jj * ROWS)
        return remote(
            grads[kv].at[rows, pl.ds(p * D, D)], cb.at[src, kv, rows],
            s3_send.at[p, kv], s3_recv.at[src, kv], {"head": p},
        )

    def share(jj, kv, src):
        return remote(
            grads[kv].at[pl.ds(SPAN + jj * ROWS, ROWS)], ob.at[src, kv],
            own_send.at[jj, kv], own_recv.at[src, kv], {"head": half * STEPS + jj},
        )

    def entropy(p, src):
        return remote(ent_ref.at[p], eb.at[src], e_send.at[p], e_recv.at[src], {"head": p})

    mine = [
        pltpu.make_async_copy(
            grads[kv].at[pl.ds(0, SPAN), pl.ds(me * D, D)], cb.at[me, kv], local.at[kv]
        )
        for kv in range(2)
    ] + [pltpu.make_async_copy(ent_ref.at[me], eb.at[me], local.at[2])]
    for jj in range(STEPS):
        @pl.when(j == jj)
        def _(jj=jj):
            for p in range(HEADS):
                @pl.when(me != p)
                def _(p=p):
                    for kv in range(2):
                        collect(p, kv, me, jj).start()
    for copy in mine:
        copy.start()
    for copy in mine:
        copy.wait()
    for p in range(HEADS):
        @pl.when(me != p)
        def _(p=p):
            for kv in range(2):
                collect(p, kv, p, p % STEPS).wait_recv()

    def summed(side):
        blocks = []
        for b in range(STEPS):
            rows = slice(b * ROWS, (b + 1) * ROWS)
            total = cb[side * STEPS, :, rows].astype(F32)
            for jj in range(1, b + 1):
                total = total + cb[side * STEPS + jj, :, rows].astype(F32)
            blocks.append(total.astype(BF16))
        return jnp.concatenate(blocks, axis=1)

    a, b = summed(0), summed(1)
    nb[0] = jnp.where(first_low, a, b)
    nb[1] = jnp.where(first_low, b, a)
    low = remote(nb.at[0], rb.at[0], s2_send.at[0], s2_recv.at[0], below)
    high = remote(nb.at[1], rb.at[1], s2_send.at[1], s2_recv.at[1], above)
    low.start()
    high.start()
    for jj in range(STEPS - 1):
        @pl.when(jj < j)
        def _(jj=jj):
            for kv in range(2):
                share(jj, kv, j).start()
    for p in range(HEADS):
        @pl.when(me != p)
        def _(p=p):
            entropy(p, me).start()
    low.wait_recv()
    high.wait_recv()
    low_part = jnp.where(own == cycle - 1, nb[1], rb[0])
    high_part = jnp.where(own == 0, jnp.zeros_like(rb[1]), rb[1])
    sb[0] = jnp.where(first_low, low_part, high_part)
    sb[1] = jnp.where(first_low, high_part, low_part)

    def deliver(p, kv, src):
        return remote(
            sb.at[p // STEPS, kv, pl.ds((p % STEPS) * ROWS, ROWS)], xb.at[kv, :, pl.ds(src * D, D)],
            s1_send.at[p, kv], s1_recv.at[src, kv], {"head": p},
        )

    for p in range(HEADS):
        @pl.when(me != p)
        def _(p=p):
            for kv in range(2):
                deliver(p, kv, me).start()
    back = [
        pltpu.make_async_copy(
            sb.at[half, kv, pl.ds(j * ROWS, ROWS)], xb.at[kv, :, pl.ds(me * D, D)], local.at[kv]
        )
        for kv in range(2)
    ]
    for copy in back:
        copy.start()
    for p in range(HEADS):
        @pl.when(me != p)
        def _(p=p):
            entropy(p, p).wait_recv()
    for n in range(HEADS // 2):
        ent_out[:, n * D : n * D + ROWS] = eb[2 * n, :, :ROWS]
        ent_out[:, n * D + ROWS : (n + 1) * D] = eb[2 * n + 1, :, :ROWS]
    ob[0] = jnp.zeros_like(ob[0])
    for jj in range(1, STEPS):
        @pl.when(jj > j)
        def _(jj=jj):
            for kv in range(2):
                share(0, kv, jj).wait_recv()

        @pl.when(jj <= j)
        def _(jj=jj):
            ob[jj] = jnp.zeros_like(ob[jj])
    for copy in back:
        copy.wait()
    for p in range(HEADS):
        @pl.when(me != p)
        def _(p=p):
            for kv in range(2):
                deliver(p, kv, p).wait_recv()
    for kv in range(2):
        total = owns[kv][...] + xb[kv].astype(F32)
        for jj in range(1, STEPS):
            total = total + ob[jj, kv].astype(F32)
        outs[kv][...] = total.astype(BF16)
    for jj in range(STEPS):
        @pl.when(j == jj)
        def _(jj=jj):
            for p in range(HEADS):
                @pl.when(me != p)
                def _(p=p):
                    for kv in range(2):
                        collect(p, kv, me, jj).wait_send()
    for p in range(HEADS):
        @pl.when(me != p)
        def _(p=p):
            entropy(p, me).wait_send()
            for kv in range(2):
                deliver(p, kv, me).wait_send()
    for jj in range(STEPS - 1):
        @pl.when(jj < j)
        def _(jj=jj):
            for kv in range(2):
                share(jj, kv, j).wait_send()
    low.wait_send()
    high.wait_send()


def vmem(count):
    return [pl.BlockSpec(memory_space=pltpu.VMEM)] * count


def body(queries, keys, values, dout, doc_lengths, span_order):
    sem = pltpu.SemaphoreType.DMA
    smem = pl.BlockSpec(memory_space=pltpu.SMEM)
    width = HEADS * D
    pair = jax.ShapeDtypeStruct((2 * SPAN, width), BF16)
    kk, vv = pl.pallas_call(
        gather_kernel,
        out_shape=(pair, pair),
        in_specs=[smem] + vmem(2),
        out_specs=vmem(2),
        scratch_shapes=[
            pltpu.VMEM((2, 2 * SPAN, D), BF16),
            pltpu.VMEM((2, 2, SPAN, D), BF16),
            pltpu.VMEM((2, 2, SPAN, D), BF16),
            pltpu.VMEM((2, 2, SPAN, D), BF16),
            sem((HEADS, 2)), sem((HEADS, 2)), sem((STEPS, 2)), sem((STEPS, 2)),
            sem((2,)), sem((2,)), sem((HEADS, 2)), sem((HEADS, 2)), sem((4,)),
        ],
        compiler_params=pltpu.CompilerParams(collective_id=0, has_side_effects=True),
    )(span_order, keys, values)

    wide = pl.BlockSpec((ROWS, width), lambda h: (0, h))
    key_block = pl.BlockSpec((2 * SPAN, D), lambda h: (0, h))
    row_block = pl.BlockSpec((ROWS, D), lambda h: (0, h))
    tokens = jax.ShapeDtypeStruct((ROWS, HEADS * width), BF16)
    own_shape = jax.ShapeDtypeStruct((ROWS, width), F32)
    out, dq, gk, gv, ok, ov, ent = pl.pallas_call(
        attend_kernel,
        grid=(HEADS,),
        out_shape=(
            tokens, tokens, pair, pair, own_shape, own_shape,
            jax.ShapeDtypeStruct((HEADS, HEADS, D), F32),
        ),
        in_specs=[
            smem, pl.BlockSpec((1, D), lambda h: (0, 0)), wide, wide, key_block, key_block,
        ],
        out_specs=(
            wide, wide, key_block, key_block, row_block, row_block,
            pl.BlockSpec((1, HEADS, D), lambda h: (h, 0, 0)),
        ),
        scratch_shapes=[pltpu.VMEM((KEYS, D), F32)],
        compiler_params=pltpu.CompilerParams(dimension_semantics=("arbitrary",)),
    )(span_order, doc_lengths.reshape(1, D), queries, dout, kk, vv)

    grad = jax.ShapeDtypeStruct((ROWS, width), BF16)
    dk, dv, ent = pl.pallas_call(
        scatter_kernel,
        out_shape=(grad, grad, jax.ShapeDtypeStruct((HEADS, 2 * SPAN), F32)),
        in_specs=[smem] + vmem(5),
        out_specs=vmem(3),
        scratch_shapes=[
            pltpu.VMEM((HEADS, 2, SPAN, D), BF16),
            pltpu.VMEM((2, 2, SPAN, D), BF16),
            pltpu.VMEM((2, 2, SPAN, D), BF16),
            pltpu.VMEM((2, 2, SPAN, D), BF16),
            pltpu.VMEM((2, ROWS, width), BF16),
            pltpu.VMEM((STEPS, 2, ROWS, width), BF16),
            pltpu.VMEM((HEADS, HEADS, D), F32),
            sem((HEADS, 2)), sem((HEADS, 2)), sem((STEPS, 2)), sem((STEPS, 2)),
            sem((2,)), sem((2,)), sem((HEADS, 2)), sem((HEADS, 2)), sem((HEADS,)), sem((HEADS,)),
            sem((3,)),
        ],
        compiler_params=pltpu.CompilerParams(collective_id=1, has_side_effects=True),
    )(span_order, gk, gv, ok, ov, ent)
    return out, ent.T, dq, dk, dv


def solution(mesh):
    rows = P(("inner", "outer", "head"), None)
    return jax.shard_map(
        body,
        mesh=mesh,
        in_specs=(rows, rows, rows, rows, P(), P()),
        out_specs=(rows, P(("inner", "outer"), "head"), rows, rows, rows),
        check_vma=False,
    )
```

```python
import math

import jax
import jax.numpy as jnp
from jax import lax
from jax.experimental import pallas as pl
from jax.experimental.pallas import tpu as pltpu
from jax.sharding import PartitionSpec as P

MESH = pl.DeviceIdType.MESH
F32 = jnp.float32
BF16 = jnp.bfloat16
NEG = -1.0e30
LN2 = math.log(2.0)

D = 128
HEADS = 8
ROWS = 64
SPAN = 256
KEYS = 320
STEPS = SPAN // ROWS
PER = 4
SPLIT = 5
SPLIT_ROWS = 3
COPY_STEPS = 2


def place():
    me = lax.axis_index("head")
    outer_size = lax.axis_size("outer")
    cycle = lax.axis_size("inner") * outer_size
    own = lax.axis_index("inner") * outer_size + lax.axis_index("outer")

    def at(index):
        return {"inner": index // outer_size, "outer": lax.rem(index, outer_size)}

    above = at(lax.rem(own + 1, cycle))
    below = at(lax.rem(own + cycle - 1, cycle))
    return me, me // STEPS, lax.rem(me, STEPS), own, cycle, above, below


def greet(me, above, below):
    barrier = pltpu.get_barrier_semaphore()
    for step in range(1, HEADS):
        pl.semaphore_signal(
            barrier, inc=1, device_id={"head": lax.rem(me + step, HEADS)}, device_id_type=MESH
        )
    pl.semaphore_signal(barrier, inc=1, device_id=above, device_id_type=MESH)
    pl.semaphore_signal(barrier, inc=1, device_id=below, device_id_type=MESH)
    pl.semaphore_wait(barrier, HEADS + 1)


def remote(src, dst, send, recv, device):
    return pltpu.make_async_remote_copy(
        src_ref=src, dst_ref=dst, send_sem=send, recv_sem=recv, device_id=device, device_id_type=MESH
    )


def kernel(
    order_ref, len_ref, q_hbm, do_hbm, k_ref, v_ref,
    out_hbm, dq_hbm, dk_ref, dv_ref, ent_out,
    bias_ref, qs, dos, outs, dqs, kk, vv, gk, gv, own_grad, pf, pb, dsb,
    hb, nb, rb, sel, cb, tnb, trb, tsel, xb, ob, es, eb,
    s1_send, s1_recv, own_send, own_recv, s2_send, s2_recv, s3_send, s3_recv,
    t1_send, t1_recv, town_send, town_recv, t2_send, t2_recv, t3_send, t3_recv,
    e_send, e_recv, local, q_sem, o_sem,
):
    me, half, j, own, cycle, above, below = place()
    ins, keep, grads = (k_ref, v_ref), (kk, vv), (gk, gv)
    first_low = order_ref[2 * own] == own
    width = HEADS * D
    loads = []
    for h in range(HEADS):
        cols = pl.ds(h * width, width)
        loads.append(pltpu.make_async_copy(q_hbm.at[:, cols], qs.at[h], q_sem.at[0, h]))
        loads.append(pltpu.make_async_copy(do_hbm.at[:, cols], dos.at[h], q_sem.at[1, h]))
    for copy in loads:
        copy.start()

    def each(action):
        for p in range(HEADS):
            @pl.when(me != p)
            def _(p=p):
                action(p)

    def branch(action):
        for jj in range(STEPS):
            @pl.when(j == jj)
            def _(jj=jj):
                action(jj)

    def spread(p, kv, src):
        return remote(
            ins[kv].at[:, pl.ds(p * D, D)], hb.at[kv, pl.ds(src * ROWS, ROWS)],
            s1_send.at[p, kv], s1_recv.at[src, kv], {"head": p},
        )

    def share(jj, kv, src):
        return remote(
            ins[kv], keep[kv].at[pl.ds(SPAN + src * ROWS, ROWS)],
            own_send.at[jj, kv], own_recv.at[src, kv], {"head": half * STEPS + jj},
        )

    def pass_on(side, kv):
        return remote(
            nb.at[side, kv], rb.at[side, kv], s2_send.at[side, kv], s2_recv.at[side, kv],
            (above, below)[side],
        )

    def deliver(p, kv, src, jj):
        rows = pl.ds(jj * ROWS, SPAN - jj * ROWS)
        return remote(
            sel.at[p // STEPS, kv, rows], keep[kv].at[rows, pl.ds(src * D, D)],
            s3_send.at[p, kv], s3_recv.at[src, kv], {"head": p},
        )

    def collect(p, kv, src, jj):
        rows = pl.ds(jj * ROWS, SPAN - jj * ROWS)
        return remote(
            grads[kv].at[rows, pl.ds(p * D, D)], cb.at[src, kv, rows],
            t3_send.at[p, kv], t3_recv.at[src, kv], {"head": p},
        )

    def share_back(jj, kv, src):
        return remote(
            grads[kv].at[pl.ds(SPAN + jj * ROWS, ROWS)], ob.at[src, kv],
            town_send.at[jj, kv], town_recv.at[src, kv], {"head": half * STEPS + jj},
        )

    def pass_back(side, kv):
        return remote(
            tnb.at[side, kv], trb.at[side, kv], t2_send.at[side, kv], t2_recv.at[side, kv],
            (below, above)[side],
        )

    def give_back(p, kv, src):
        return remote(
            tsel.at[p // STEPS, kv, pl.ds((p % STEPS) * ROWS, ROWS)],
            xb.at[kv, :, pl.ds(src * D, D)],
            t1_send.at[p, kv], t1_recv.at[src, kv], {"head": p},
        )

    def entropy_to(p, src):
        return remote(es.at[p], eb.at[src], e_send.at[p], e_recv.at[src], {"head": p})

    greet(me, above, below)
    for kv in range(2):
        each(lambda p: spread(p, kv, me).start())
    mine = [
        pltpu.make_async_copy(
            ins[kv].at[:, pl.ds(me * D, D)], hb.at[kv, pl.ds(me * ROWS, ROWS)], local.at[kv]
        )
        for kv in range(2)
    ] + [
        pltpu.make_async_copy(
            ins[kv], keep[kv].at[pl.ds(SPAN + j * ROWS, ROWS)], local.at[2 + kv]
        )
        for kv in range(2)
    ]
    for copy in mine:
        copy.start()

    start_pos = order_ref[2 * own + half] * SPAN + j * ROWS
    lens = jnp.broadcast_to(len_ref[...], (D, D)).astype(F32)
    row = lax.broadcasted_iota(jnp.int32, (D, D), 0)
    col = lax.broadcasted_iota(jnp.int32, (D, D), 1)
    starts = jnp.sum(jnp.where(col < row, lens, 0.0), axis=1, keepdims=True)
    pos = (start_pos + lax.rem(col, ROWS)).astype(F32)
    found = jnp.max(jnp.where(starts <= pos, starts, 0.0), axis=0, keepdims=True)
    first = found - (start_pos - SPAN).astype(F32)
    key = lax.broadcasted_iota(jnp.int32, (KEYS, D), 0)
    query = lax.rem(lax.broadcasted_iota(jnp.int32, (KEYS, D), 1), ROWS)
    allowed = (key.astype(F32) >= first) & (key <= query + SPAN)
    bias_ref[...] = jnp.where(allowed, 0.0, NEG)
    for copy in mine:
        copy.wait()

    for kv in range(2):
        each(lambda p: spread(p, kv, p).wait_recv())
        a, b = hb[kv, :SPAN], hb[kv, SPAN:]
        nb[0, kv] = jnp.where(first_low, a, b)
        nb[1, kv] = jnp.where(first_low, b, a)
        pass_on(0, kv).start()
        pass_on(1, kv).start()
    for kv in range(2):
        for jj in range(1, STEPS):
            @pl.when(j < jj)
            def _(jj=jj):
                share(jj, kv, j).start()
    back = []
    for kv in range(2):
        pass_on(0, kv).wait_recv()
        pass_on(1, kv).wait_recv()
        prev_low = rb[0, kv]
        prev_high = jnp.where(own == cycle - 1, nb[0, kv], rb[1, kv])
        sel[0, kv] = jnp.where(first_low, prev_low, prev_high)
        sel[1, kv] = jnp.where(first_low, prev_high, prev_low)
        each(lambda p: deliver(p, kv, me, p % STEPS).start())
        copy = pltpu.make_async_copy(
            sel.at[half, kv], keep[kv].at[pl.ds(0, SPAN), pl.ds(me * D, D)], local.at[kv]
        )
        copy.start()
        back.append(copy)

    def wait_own(kv):
        for jj in range(STEPS - 1):
            @pl.when(jj < j)
            def _(jj=jj):
                share(0, kv, jj).wait_recv()

    scale = 1.0 / math.sqrt(D)
    nt = (((1,), (1,)), ((), ()))
    nn = (((1,), (0,)), ((), ()))
    lanes = PER * ROWS
    rows = pl.multiple_of(j * ROWS, ROWS)
    window = pl.ds(rows, KEYS)
    sub = lax.broadcasted_iota(jnp.int32, (HEADS, D), 0)

    def columns(h):
        return pl.ds(pl.multiple_of(h * D, D), D)

    def stacked(ref, h, chunk):
        return jnp.concatenate(
            [ref[h, :, g * D : (g + 1) * D] for g in range(chunk * PER, (chunk + 1) * PER)], axis=0
        )

    def arrive(step, h, kv):
        @pl.when(step > 0)
        def _():
            branch(lambda jj: deliver(h, kv, h, jj).wait_recv())

    def leave(step, h, kv):
        @pl.when(step > 0)
        def _():
            branch(lambda jj: collect(h, kv, me, jj).start())

    def store_grad(kv, h, total):
        grads[kv][pl.ds(rows, SPAN), columns(h)] = total[:SPAN].astype(BF16)
        own_grad[kv, :, columns(h)] = total[SPAN:]

    def score_step(step, carry):
        h = lax.rem(me + step, HEADS)
        arrive(step, h, 0)
        k5 = kk[window, columns(h)]
        bias = jnp.concatenate([bias_ref[...]] * (lanes // D), axis=1)
        ent = jnp.zeros((HEADS, D), F32)
        dv = jnp.zeros((KEYS, D), F32)
        for chunk in range(HEADS // PER):
            at = slice(chunk * lanes, (chunk + 1) * lanes)
            q, do = stacked(qs, h, chunk), stacked(dos, h, chunk)
            t = lax.dot_general(k5, q, nt, preferred_element_type=F32) * (scale / LN2) + bias
            u = t - jnp.max(t, axis=0, keepdims=True)
            e = jnp.exp2(u)
            total = jnp.sum(e, axis=0, keepdims=True)
            p = e * (1.0 / total)
            spread_sum = jnp.sum(p * u, axis=0, keepdims=True)
            entropy = LN2 * (jnp.log2(total) - spread_sum)
            pf[h, :, at] = p
            rounded = p.astype(BF16)
            pb[h, :, at] = rounded
            dv = dv + lax.dot_general(rounded, do, nn, preferred_element_type=F32)
            for n in range(PER // 2):
                pair = jnp.broadcast_to(entropy[:, n * D : (n + 1) * D], (HEADS, D))
                g = chunk * PER + 2 * n
                ent = jnp.where(sub == g, pair, ent)
                ent = jnp.where(sub == g + 1, pltpu.roll(pair, ROWS, 1), ent)
        es[h] = ent
        store_grad(1, h, dv)
        leave(step, h, 1)

        @pl.when(step > 0)
        def _():
            entropy_to(h, me).start()

        return carry

    def slope_step(step, carry):
        h = lax.rem(me + step, HEADS)
        arrive(step, h, 1)
        v5 = vv[window, columns(h)]
        dk = jnp.zeros((KEYS, D), F32)
        for chunk in range(HEADS // PER):
            at = slice(chunk * lanes, (chunk + 1) * lanes)
            q, do = stacked(qs, h, chunk), stacked(dos, h, chunk)
            dp = lax.dot_general(v5, do, nt, preferred_element_type=F32)
            p = pf[h, :, at]
            delta = jnp.sum(p * dp, axis=0, keepdims=True)
            ds = (p * ((dp - delta) * scale)).astype(BF16)
            dsb[h, :, at] = ds
            dk = dk + lax.dot_general(ds, q, nn, preferred_element_type=F32)
        store_grad(0, h, dk)
        leave(step, h, 0)
        return carry

    def stores(h):
        cols = pl.ds(pl.multiple_of(h * width, width), width)
        return (
            pltpu.make_async_copy(outs.at[h], out_hbm.at[:, cols], o_sem.at[0, h]),
            pltpu.make_async_copy(dqs.at[h], dq_hbm.at[:, cols], o_sem.at[1, h]),
        )

    def row_step(h, carry):
        k5t, v5t = kk[window, columns(h)].T, vv[window, columns(h)].T
        for chunk in range(HEADS // PER):
            at = slice(chunk * lanes, (chunk + 1) * lanes)
            out = lax.dot_general(v5t, pb[h, :, at], nn, preferred_element_type=F32).T
            dq = lax.dot_general(k5t, dsb[h, :, at], nn, preferred_element_type=F32).T
            for n in range(PER):
                g = chunk * PER + n
                outs[h, :, g * D : (g + 1) * D] = out[n * ROWS : (n + 1) * ROWS].astype(BF16)
                dqs[h, :, g * D : (g + 1) * D] = dq[n * ROWS : (n + 1) * ROWS].astype(BF16)
        for copy in stores(h):
            copy.start()
        return carry

    def summed(kv):
        sides = []
        for side in range(2):
            blocks = []
            for b in range(STEPS):
                at = slice(b * ROWS, (b + 1) * ROWS)
                total = cb[side * STEPS, kv, at].astype(F32)
                for jj in range(1, b + 1):
                    total = total + cb[side * STEPS + jj, kv, at].astype(F32)
                blocks.append(total.astype(BF16))
            sides.append(jnp.concatenate(blocks, axis=0))
        tnb[0, kv] = jnp.where(first_low, sides[0], sides[1])
        tnb[1, kv] = jnp.where(first_low, sides[1], sides[0])

    def keep_mine(kv):
        return pltpu.make_async_copy(
            grads[kv].at[pl.ds(0, SPAN), pl.ds(me * D, D)], cb.at[me, kv], local.at[5 + kv]
        )

    def send_sums(kv):
        each(lambda p: collect(p, kv, p, p % STEPS).wait_recv())
        keep_mine(kv).wait()
        summed(kv)
        pass_back(0, kv).start()
        pass_back(1, kv).start()

    def send_shares(kv):
        for jj in range(STEPS - 1):
            @pl.when(jj < j)
            def _(jj=jj):
                share_back(jj, kv, j).start()

    def keep_given(kv):
        return pltpu.make_async_copy(
            tsel.at[half, kv, pl.ds(j * ROWS, ROWS)], xb.at[kv, :, pl.ds(me * D, D)],
            local.at[2 + kv],
        )

    def send_given(kv):
        pass_back(0, kv).wait_recv()
        pass_back(1, kv).wait_recv()
        low_part = jnp.where(own == cycle - 1, tnb[1, kv], trb[0, kv])
        high_part = jnp.where(own == 0, jnp.zeros_like(trb[1, kv]), trb[1, kv])
        tsel[0, kv] = jnp.where(first_low, low_part, high_part)
        tsel[1, kv] = jnp.where(first_low, high_part, low_part)
        each(lambda p: give_back(p, kv, me).start())
        keep_given(kv).start()

    def finish(kv, dst):
        ob[0, kv] = jnp.zeros_like(ob[0, kv])
        for jj in range(1, STEPS):
            @pl.when(jj > j)
            def _(jj=jj):
                share_back(0, kv, jj).wait_recv()

            @pl.when(jj <= j)
            def _(jj=jj):
                ob[jj, kv] = jnp.zeros_like(ob[jj, kv])
        keep_given(kv).wait()
        each(lambda p: give_back(p, kv, p).wait_recv())
        total = own_grad[kv] + xb[kv].astype(F32)
        for jj in range(1, STEPS):
            total = total + ob[jj, kv].astype(F32)
        dst[...] = total.astype(BF16)

    for copy in loads:
        copy.wait()
    wait_own(0)
    back[0].wait()
    lax.fori_loop(0, HEADS, score_step, 0)
    keep_mine(1).start()
    send_shares(1)
    wait_own(1)
    back[1].wait()
    lax.fori_loop(0, SPLIT, slope_step, 0)
    send_sums(1)
    lax.fori_loop(SPLIT, HEADS, slope_step, 0)
    keep_mine(0).start()
    send_shares(0)
    lax.fori_loop(0, SPLIT_ROWS, row_step, 0)
    send_sums(0)
    send_given(1)
    lax.fori_loop(SPLIT_ROWS, HEADS, row_step, 0)
    send_given(0)
    finish(1, dv_ref)
    local_ent = pltpu.make_async_copy(es.at[me], eb.at[me], local.at[4])
    local_ent.start()
    local_ent.wait()
    each(lambda p: entropy_to(p, p).wait_recv())
    for n in range(HEADS // 2):
        ent_out[:, n * D : n * D + ROWS] = eb[2 * n, :, :ROWS]
        ent_out[:, n * D + ROWS : (n + 1) * D] = eb[2 * n + 1, :, :ROWS]
    finish(0, dk_ref)
    for kv in range(2):
        branch(lambda jj: each(lambda p: collect(p, kv, me, jj).wait_send()))

        def sent(p):
            spread(p, kv, me).wait_send()
            deliver(p, kv, me, p % STEPS).wait_send()
            give_back(p, kv, me).wait_send()

        each(sent)
        for jj in range(STEPS):
            if jj > 0:
                @pl.when(j < jj)
                def _(jj=jj):
                    share(jj, kv, j).wait_send()

            if jj < STEPS - 1:
                @pl.when(jj < j)
                def _(jj=jj):
                    share_back(jj, kv, j).wait_send()

        for side in range(2):
            pass_on(side, kv).wait_send()
            pass_back(side, kv).wait_send()
    each(lambda p: entropy_to(p, me).wait_send())
    for h in range(HEADS):
        for copy in stores(h):
            copy.wait()


def copy_kernel(*refs):
    count = len(refs) // 2
    for src, dst in zip(refs[:count], refs[count:]):
        dst[...] = src[...]


def body(queries, keys, values, dout, doc_lengths, span_order):
    sem = pltpu.SemaphoreType.DMA
    smem = pl.BlockSpec(memory_space=pltpu.SMEM)
    hbm = pl.BlockSpec(memory_space=pl.ANY)
    whole = pl.BlockSpec(memory_space=pltpu.VMEM)
    width = HEADS * D
    lanes = HEADS * ROWS
    tokens = jax.ShapeDtypeStruct((ROWS, HEADS * width), BF16)
    grad = jax.ShapeDtypeStruct((ROWS, width), BF16)
    entropy = jax.ShapeDtypeStruct((HEADS, 2 * SPAN), F32)
    side = pltpu.VMEM((2, 2, SPAN, D), BF16)
    results = pl.pallas_call(
        kernel,
        out_shape=(tokens, tokens, grad, grad, entropy),
        in_specs=[smem, whole, hbm, hbm, whole, whole],
        out_specs=(hbm, hbm, whole, whole, whole),
        scratch_shapes=[
            pltpu.VMEM((KEYS, D), F32),
            pltpu.VMEM((HEADS, ROWS, width), BF16),
            pltpu.VMEM((HEADS, ROWS, width), BF16),
            pltpu.VMEM((HEADS, ROWS, width), BF16),
            pltpu.VMEM((HEADS, ROWS, width), BF16),
            pltpu.VMEM((2 * SPAN, width), BF16),
            pltpu.VMEM((2 * SPAN, width), BF16),
            pltpu.VMEM((2 * SPAN, width), BF16),
            pltpu.VMEM((2 * SPAN, width), BF16),
            pltpu.VMEM((2, ROWS, width), F32),
            pltpu.VMEM((HEADS, KEYS, lanes), F32),
            pltpu.VMEM((HEADS, KEYS, lanes), BF16),
            pltpu.VMEM((HEADS, KEYS, lanes), BF16),
            pltpu.VMEM((2, 2 * SPAN, D), BF16),
            side, side, side,
            pltpu.VMEM((HEADS, 2, SPAN, D), BF16),
            side, side, side,
            pltpu.VMEM((2, ROWS, width), BF16),
            pltpu.VMEM((STEPS, 2, ROWS, width), BF16),
            pltpu.VMEM((HEADS, HEADS, D), F32),
            pltpu.VMEM((HEADS, HEADS, D), F32),
            sem((HEADS, 2)), sem((HEADS, 2)), sem((STEPS, 2)), sem((STEPS, 2)),
            sem((2, 2)), sem((2, 2)), sem((HEADS, 2)), sem((HEADS, 2)),
            sem((HEADS, 2)), sem((HEADS, 2)), sem((STEPS, 2)), sem((STEPS, 2)),
            sem((2, 2)), sem((2, 2)), sem((HEADS, 2)), sem((HEADS, 2)),
            sem((HEADS,)), sem((HEADS,)), sem((7,)), sem((2, HEADS)), sem((2, HEADS)),
        ],
        compiler_params=pltpu.CompilerParams(collective_id=0, has_side_effects=True),
    )(span_order, doc_lengths.reshape(1, D), queries, dout, keys, values)
    if COPY_STEPS:
        blocks = [
            pl.BlockSpec((s.shape[0], s.shape[1] // COPY_STEPS), lambda n: (0, n))
            for s in (tokens, tokens, grad, grad, entropy)
        ]
        results = pl.pallas_call(
            copy_kernel,
            grid=(COPY_STEPS,),
            out_shape=(tokens, tokens, grad, grad, entropy),
            in_specs=blocks,
            out_specs=tuple(blocks),
        )(*results)
    out, dq, dk, dv, ent = results
    return out, ent.T, dq, dk, dv


def solution(mesh):
    rows = P(("inner", "outer", "head"), None)
    return jax.shard_map(
        body,
        mesh=mesh,
        in_specs=(rows, rows, rows, rows, P(), P()),
        out_specs=(rows, P(("inner", "outer"), "head"), rows, rows, rows),
        check_vma=False,
    )
```

```python
import math

import jax
import jax.numpy as jnp
from jax import lax
from jax.experimental import pallas as pl
from jax.experimental.pallas import tpu as pltpu
from jax.sharding import PartitionSpec as P

MESH = pl.DeviceIdType.MESH
F32 = jnp.float32
BF16 = jnp.bfloat16
NEG = -1.0e30
LN2 = math.log(2.0)

D = 128
HEADS = 8
ROWS = 64
SPAN = 256
KEYS = 320
STEPS = SPAN // ROWS
PER = 4
SPLIT = 6
SPLIT_ROWS = 3
VMEM_LIMIT = 40 << 20


def place():
    me = lax.axis_index("head")
    outer_size = lax.axis_size("outer")
    cycle = lax.axis_size("inner") * outer_size
    own = lax.axis_index("inner") * outer_size + lax.axis_index("outer")

    def at(index):
        return {"inner": index // outer_size, "outer": lax.rem(index, outer_size)}

    above = at(lax.rem(own + 1, cycle))
    below = at(lax.rem(own + cycle - 1, cycle))
    return me, me // STEPS, lax.rem(me, STEPS), own, cycle, above, below


def greet(me, above, below):
    barrier = pltpu.get_barrier_semaphore()
    for step in range(1, HEADS):
        pl.semaphore_signal(
            barrier, inc=1, device_id={"head": lax.rem(me + step, HEADS)}, device_id_type=MESH
        )
    pl.semaphore_signal(barrier, inc=1, device_id=above, device_id_type=MESH)
    pl.semaphore_signal(barrier, inc=1, device_id=below, device_id_type=MESH)
    pl.semaphore_wait(barrier, HEADS + 1)


def remote(src, dst, send, recv, device):
    return pltpu.make_async_remote_copy(
        src_ref=src, dst_ref=dst, send_sem=send, recv_sem=recv, device_id=device, device_id_type=MESH
    )


def kernel(
    order_hbm, len_hbm, q_hbm, do_hbm, k_ref, v_ref,
    outs, dqs, dk_ref, dv_ref, ent_out,
    order_ref, len_ref, bias_ref, qs, dos, kk, vv, gk, gv, own_grad, pf, pb, dsb,
    hb, nb, rb, sel, cb, tnb, trb, tsel, xb, ob, es, eb,
    s1_send, s1_recv, own_send, own_recv, s2_send, s2_recv, s3_send, s3_recv,
    t1_send, t1_recv, town_send, town_recv, t2_send, t2_recv, t3_send, t3_recv,
    e_send, e_recv, local, q_sem,
):
    me, half, j, own, cycle, above, below = place()
    ins, keep, grads = (k_ref, v_ref), (kk, vv), (gk, gv)
    width = HEADS * D
    loads = []
    facts = [
        pltpu.make_async_copy(order_hbm, order_ref, local.at[11]),
        pltpu.make_async_copy(len_hbm, len_ref, local.at[12]),
    ]
    for copy in facts:
        copy.start()
    for h in range(HEADS):
        cols = pl.ds(h * width, width)
        loads.append(pltpu.make_async_copy(q_hbm.at[:, cols], qs.at[h], q_sem.at[0, h]))
        loads.append(pltpu.make_async_copy(do_hbm.at[:, cols], dos.at[h], q_sem.at[1, h]))
    for copy in loads:
        copy.start()

    def each(action):
        for p in range(HEADS):
            @pl.when(me != p)
            def _(p=p):
                action(p)

    def branch(action):
        for jj in range(STEPS):
            @pl.when(j == jj)
            def _(jj=jj):
                action(jj)

    def later(action):
        for jj in range(1, STEPS):
            @pl.when(j == jj)
            def _(jj=jj):
                action(jj)

    def spread(p, kv, src):
        return remote(
            ins[kv].at[:, pl.ds(p * D, D)], hb.at[kv, pl.ds(src * ROWS, ROWS)],
            s1_send.at[p, kv], s1_recv.at[src, kv], {"head": p},
        )

    def share(p, kv, src, jj):
        return remote(
            hb.at[kv, pl.ds((p // STEPS) * SPAN, jj * ROWS)],
            keep[kv].at[pl.ds(SPAN, jj * ROWS), pl.ds(src * D, D)],
            own_send.at[p, kv], own_recv.at[src, kv], {"head": p},
        )

    def share_mine(kv, jj):
        return pltpu.make_async_copy(
            hb.at[kv, pl.ds(half * SPAN, jj * ROWS)],
            keep[kv].at[pl.ds(SPAN, jj * ROWS), pl.ds(me * D, D)], local.at[7 + kv],
        )

    def pass_on(side, kv):
        return remote(
            nb.at[side, kv], rb.at[side, kv], s2_send.at[side, kv], s2_recv.at[side, kv],
            (above, below)[side],
        )

    def deliver(p, kv, src, jj):
        rows = pl.ds(jj * ROWS, SPAN - jj * ROWS)
        return remote(
            sel.at[p // STEPS, kv, rows], keep[kv].at[rows, pl.ds(src * D, D)],
            s3_send.at[p, kv], s3_recv.at[src, kv], {"head": p},
        )

    def collect(p, kv, src, jj):
        rows = pl.ds(jj * ROWS, SPAN - jj * ROWS)
        return remote(
            grads[kv].at[rows, pl.ds(p * D, D)], cb.at[src, kv, rows],
            t3_send.at[p, kv], t3_recv.at[src, kv], {"head": p},
        )

    def share_back(p, kv, src, jj):
        return remote(
            grads[kv].at[pl.ds(SPAN, jj * ROWS), pl.ds(p * D, D)],
            ob.at[src, kv, pl.ds(0, jj * ROWS)],
            town_send.at[p, kv], town_recv.at[src, kv], {"head": p},
        )

    def share_back_mine(kv, jj):
        return pltpu.make_async_copy(
            grads[kv].at[pl.ds(SPAN, jj * ROWS), pl.ds(me * D, D)],
            ob.at[me, kv, pl.ds(0, jj * ROWS)], local.at[9 + kv],
        )

    def pass_back(side, kv):
        return remote(
            tnb.at[side, kv], trb.at[side, kv], t2_send.at[side, kv], t2_recv.at[side, kv],
            (below, above)[side],
        )

    def give_back(p, kv, src):
        return remote(
            tsel.at[p // STEPS, kv, pl.ds((p % STEPS) * ROWS, ROWS)],
            xb.at[kv, :, pl.ds(src * D, D)],
            t1_send.at[p, kv], t1_recv.at[src, kv], {"head": p},
        )

    def entropy_to(p, src):
        return remote(es.at[p], eb.at[src], e_send.at[p], e_recv.at[src], {"head": p})

    greet(me, above, below)
    for kv in range(2):
        each(lambda p: spread(p, kv, me).start())
    mine = [
        pltpu.make_async_copy(
            ins[kv].at[:, pl.ds(me * D, D)], hb.at[kv, pl.ds(me * ROWS, ROWS)], local.at[kv]
        )
        for kv in range(2)
    ] + [
        pltpu.make_async_copy(
            ins[kv], keep[kv].at[pl.ds(SPAN + j * ROWS, ROWS)], local.at[2 + kv]
        )
        for kv in range(2)
    ]
    for copy in mine:
        copy.start()

    for copy in facts:
        copy.wait()
    first_low = order_ref[2 * own] == own
    start_pos = order_ref[2 * own + half] * SPAN + j * ROWS
    lens = jnp.broadcast_to(len_ref[...], (D, D)).astype(F32)
    row = lax.broadcasted_iota(jnp.int32, (D, D), 0)
    col = lax.broadcasted_iota(jnp.int32, (D, D), 1)
    starts = jnp.sum(jnp.where(col < row, lens, 0.0), axis=1, keepdims=True)
    pos = (start_pos + lax.rem(col, ROWS)).astype(F32)
    found = jnp.max(jnp.where(starts <= pos, starts, 0.0), axis=0, keepdims=True)
    first = found - (start_pos - SPAN).astype(F32)
    key = lax.broadcasted_iota(jnp.int32, (KEYS, D), 0)
    query = lax.rem(lax.broadcasted_iota(jnp.int32, (KEYS, D), 1), ROWS)
    allowed = (key.astype(F32) >= first) & (key <= query + SPAN)
    bias_ref[...] = jnp.where(allowed, 0.0, NEG)
    for copy in mine:
        copy.wait()

    for kv in range(2):
        each(lambda p: spread(p, kv, p).wait_recv())
        a, b = hb[kv, :SPAN], hb[kv, SPAN:]
        nb[0, kv] = jnp.where(first_low, a, b)
        nb[1, kv] = jnp.where(first_low, b, a)
        pass_on(0, kv).start()
        pass_on(1, kv).start()
    for kv in range(2):
        later(lambda jj: share_mine(kv, jj).start())
        each(lambda p: share(p, kv, me, p % STEPS).start() if p % STEPS else None)
    back = []
    for kv in range(2):
        pass_on(0, kv).wait_recv()
        pass_on(1, kv).wait_recv()
        prev_low = rb[0, kv]
        prev_high = jnp.where(own == cycle - 1, nb[0, kv], rb[1, kv])
        sel[0, kv] = jnp.where(first_low, prev_low, prev_high)
        sel[1, kv] = jnp.where(first_low, prev_high, prev_low)
        each(lambda p: deliver(p, kv, me, p % STEPS).start())
        copy = pltpu.make_async_copy(
            sel.at[half, kv], keep[kv].at[pl.ds(0, SPAN), pl.ds(me * D, D)], local.at[kv]
        )
        copy.start()
        back.append(copy)

    scale = 1.0 / math.sqrt(D)
    nt = (((1,), (1,)), ((), ()))
    nn = (((1,), (0,)), ((), ()))
    lanes = PER * ROWS
    rows = pl.multiple_of(j * ROWS, ROWS)
    window = pl.ds(rows, KEYS)
    sub = lax.broadcasted_iota(jnp.int32, (HEADS, D), 0)

    def columns(h):
        return pl.ds(pl.multiple_of(h * D, D), D)

    def stacked(ref, h, chunk):
        return jnp.concatenate(
            [ref[h, :, g * D : (g + 1) * D] for g in range(chunk * PER, (chunk + 1) * PER)], axis=0
        )

    def arrive(step, h, kv):
        @pl.when(step > 0)
        def _():
            branch(lambda jj: deliver(h, kv, h, jj).wait_recv())
            later(lambda jj: share(h, kv, h, jj).wait_recv())

    def leave(step, h, kv):
        @pl.when(step > 0)
        def _():
            branch(lambda jj: collect(h, kv, me, jj).start())

    def store_grad(kv, h, total):
        grads[kv][pl.ds(rows, SPAN), columns(h)] = total[:SPAN].astype(BF16)
        own_grad[kv, :, columns(h)] = total[SPAN:]

    def score_step(step, carry):
        h = lax.rem(me + step, HEADS)
        arrive(step, h, 0)
        k5 = kk[window, columns(h)]
        bias = jnp.concatenate([bias_ref[...]] * (lanes // D), axis=1)
        ent = jnp.zeros((HEADS, D), F32)
        dv = jnp.zeros((KEYS, D), F32)
        for chunk in range(HEADS // PER):
            at = slice(chunk * lanes, (chunk + 1) * lanes)
            q, do = stacked(qs, h, chunk), stacked(dos, h, chunk)
            t = lax.dot_general(k5, q, nt, preferred_element_type=F32) * (scale / LN2) + bias
            u = t - jnp.max(t, axis=0, keepdims=True)
            e = jnp.exp2(u)
            total = jnp.sum(e, axis=0, keepdims=True)
            p = e * (1.0 / total)
            spread_sum = jnp.sum(p * u, axis=0, keepdims=True)
            entropy = LN2 * (jnp.log2(total) - spread_sum)
            pf[h, :, at] = p
            rounded = p.astype(BF16)
            pb[h, :, at] = rounded
            dv = dv + lax.dot_general(rounded, do, nn, preferred_element_type=F32)
            for n in range(PER // 2):
                pair = jnp.broadcast_to(entropy[:, n * D : (n + 1) * D], (HEADS, D))
                g = chunk * PER + 2 * n
                ent = jnp.where(sub == g, pair, ent)
                ent = jnp.where(sub == g + 1, pltpu.roll(pair, ROWS, 1), ent)
        es[h] = ent
        store_grad(1, h, dv)
        leave(step, h, 1)

        @pl.when(step > 0)
        def _():
            entropy_to(h, me).start()

        return carry

    def slope_step(step, carry):
        h = lax.rem(me + step, HEADS)
        arrive(step, h, 1)
        v5 = vv[window, columns(h)]
        dk = jnp.zeros((KEYS, D), F32)
        for chunk in range(HEADS // PER):
            at = slice(chunk * lanes, (chunk + 1) * lanes)
            q, do = stacked(qs, h, chunk), stacked(dos, h, chunk)
            dp = lax.dot_general(v5, do, nt, preferred_element_type=F32)
            p = pf[h, :, at]
            delta = jnp.sum(p * dp, axis=0, keepdims=True)
            ds = (p * ((dp - delta) * scale)).astype(BF16)
            dsb[h, :, at] = ds
            dk = dk + lax.dot_general(ds, q, nn, preferred_element_type=F32)
        store_grad(0, h, dk)
        leave(step, h, 0)
        return carry

    def row_step(h, carry):
        k5t, v5t = kk[window, columns(h)].T, vv[window, columns(h)].T
        for chunk in range(HEADS // PER):
            at = slice(chunk * lanes, (chunk + 1) * lanes)
            out = lax.dot_general(v5t, pb[h, :, at], nn, preferred_element_type=F32).T
            dq = lax.dot_general(k5t, dsb[h, :, at], nn, preferred_element_type=F32).T
            for n in range(PER):
                g = chunk * PER + n
                outs[h, :, g * D : (g + 1) * D] = out[n * ROWS : (n + 1) * ROWS].astype(BF16)
                dqs[h, :, g * D : (g + 1) * D] = dq[n * ROWS : (n + 1) * ROWS].astype(BF16)
        return carry

    def summed(kv):
        sides = []
        for side in range(2):
            blocks = []
            for b in range(STEPS):
                at = slice(b * ROWS, (b + 1) * ROWS)
                total = cb[side * STEPS, kv, at].astype(F32)
                for jj in range(1, b + 1):
                    total = total + cb[side * STEPS + jj, kv, at].astype(F32)
                blocks.append(total.astype(BF16))
            sides.append(jnp.concatenate(blocks, axis=0))
        tnb[0, kv] = jnp.where(first_low, sides[0], sides[1])
        tnb[1, kv] = jnp.where(first_low, sides[1], sides[0])

    def keep_mine(kv):
        return pltpu.make_async_copy(
            grads[kv].at[pl.ds(0, SPAN), pl.ds(me * D, D)], cb.at[me, kv], local.at[5 + kv]
        )

    def send_sums(kv):
        each(lambda p: collect(p, kv, p, p % STEPS).wait_recv())
        keep_mine(kv).wait()
        summed(kv)
        pass_back(0, kv).start()
        pass_back(1, kv).start()

    def send_shares(kv):
        later(lambda jj: share_back_mine(kv, jj).start())
        later(lambda jj: each(lambda p: share_back(p, kv, me, jj).start()))

    def own_sum(kv, side):
        blocks = []
        for b in range(STEPS):
            at = slice(b * ROWS, (b + 1) * ROWS)
            total = jnp.zeros((ROWS, D), F32)
            for jj in range(b + 1, STEPS):
                total = total + ob[side * STEPS + jj, kv, at].astype(F32)
            blocks.append(total)
        return jnp.concatenate(blocks, axis=0)

    def keep_given(kv):
        return pltpu.make_async_copy(
            tsel.at[half, kv, pl.ds(j * ROWS, ROWS)], xb.at[kv, :, pl.ds(me * D, D)],
            local.at[2 + kv],
        )

    def send_given(kv):
        each(lambda p: share_back(p, kv, p, p % STEPS).wait_recv() if p % STEPS else None)
        later(lambda jj: share_back_mine(kv, jj).wait())
        pass_back(0, kv).wait_recv()
        pass_back(1, kv).wait_recv()
        low_part = jnp.where(own == cycle - 1, tnb[1, kv], trb[0, kv]).astype(F32)
        high_part = jnp.where(own == 0, jnp.zeros_like(trb[1, kv]), trb[1, kv]).astype(F32)
        first_part = jnp.where(first_low, low_part, high_part) + own_sum(kv, 0)
        second_part = jnp.where(first_low, high_part, low_part) + own_sum(kv, 1)
        tsel[0, kv] = first_part.astype(BF16)
        tsel[1, kv] = second_part.astype(BF16)
        each(lambda p: give_back(p, kv, me).start())
        keep_given(kv).start()

    def finish(kv, dst):
        keep_given(kv).wait()
        each(lambda p: give_back(p, kv, p).wait_recv())
        dst[...] = (own_grad[kv] + xb[kv].astype(F32)).astype(BF16)

    for copy in loads:
        copy.wait()
    back[0].wait()
    later(lambda jj: share_mine(0, jj).wait())
    lax.fori_loop(0, HEADS, score_step, 0)
    keep_mine(1).start()
    send_shares(1)
    back[1].wait()
    later(lambda jj: share_mine(1, jj).wait())
    lax.fori_loop(0, SPLIT, slope_step, 0)
    send_sums(1)
    lax.fori_loop(SPLIT, HEADS, slope_step, 0)
    keep_mine(0).start()
    send_shares(0)
    lax.fori_loop(0, SPLIT_ROWS, row_step, 0)
    send_sums(0)
    send_given(1)
    lax.fori_loop(SPLIT_ROWS, HEADS, row_step, 0)
    send_given(0)
    finish(1, dv_ref)
    local_ent = pltpu.make_async_copy(es.at[me], eb.at[me], local.at[4])
    local_ent.start()
    local_ent.wait()
    each(lambda p: entropy_to(p, p).wait_recv())
    for n in range(HEADS // 2):
        ent_out[:, n * D : n * D + ROWS] = eb[2 * n, :, :ROWS]
        ent_out[:, n * D + ROWS : (n + 1) * D] = eb[2 * n + 1, :, :ROWS]
    finish(0, dk_ref)
    for kv in range(2):
        branch(lambda jj: each(lambda p: collect(p, kv, me, jj).wait_send()))

        def sent(p):
            spread(p, kv, me).wait_send()
            deliver(p, kv, me, p % STEPS).wait_send()
            give_back(p, kv, me).wait_send()
            if p % STEPS:
                share(p, kv, me, p % STEPS).wait_send()

        each(sent)
        later(lambda jj: each(lambda p: share_back(p, kv, me, jj).wait_send()))
        for side in range(2):
            pass_on(side, kv).wait_send()
            pass_back(side, kv).wait_send()
    each(lambda p: entropy_to(p, me).wait_send())


def write_kernel(outs, dqs, dk, dv, ent, out_hbm, dq_hbm, dk_hbm, dv_hbm, ent_hbm, sems):
    width = HEADS * D
    copies = [
        pltpu.make_async_copy(src, dst, sems.at[n])
        for n, (src, dst) in enumerate(((dk, dk_hbm), (dv, dv_hbm), (ent, ent_hbm)))
    ]
    for h in range(HEADS):
        cols = pl.ds(h * width, width)
        copies.append(pltpu.make_async_copy(outs.at[h], out_hbm.at[:, cols], sems.at[3 + 2 * h]))
        copies.append(pltpu.make_async_copy(dqs.at[h], dq_hbm.at[:, cols], sems.at[4 + 2 * h]))
    for copy in copies:
        copy.start()
    for copy in copies:
        copy.wait()


def body(queries, keys, values, dout, doc_lengths, span_order):
    sem = pltpu.SemaphoreType.DMA
    hbm = pl.BlockSpec(memory_space=pl.ANY)
    whole = pl.BlockSpec(memory_space=pltpu.VMEM)
    width = HEADS * D
    lanes = HEADS * ROWS
    stacked = jax.ShapeDtypeStruct((HEADS, ROWS, width), BF16)
    tokens = jax.ShapeDtypeStruct((ROWS, HEADS * width), BF16)
    grad = jax.ShapeDtypeStruct((ROWS, width), BF16)
    entropy = jax.ShapeDtypeStruct((HEADS, 2 * SPAN), F32)
    side = pltpu.VMEM((2, 2, SPAN, D), BF16)
    results = pl.pallas_call(
        kernel,
        out_shape=(stacked, stacked, grad, grad, entropy),
        in_specs=[pl.BlockSpec(memory_space=pltpu.HBM)] * 6,
        out_specs=(whole, whole, whole, whole, whole),
        scratch_shapes=[
            pltpu.SMEM((span_order.shape[0],), jnp.int32),
            pltpu.VMEM((1, D), jnp.int32),
            pltpu.VMEM((KEYS, D), F32),
            pltpu.VMEM((HEADS, ROWS, width), BF16),
            pltpu.VMEM((HEADS, ROWS, width), BF16),
            pltpu.VMEM((2 * SPAN, width), BF16),
            pltpu.VMEM((2 * SPAN, width), BF16),
            pltpu.VMEM((2 * SPAN, width), BF16),
            pltpu.VMEM((2 * SPAN, width), BF16),
            pltpu.VMEM((2, ROWS, width), F32),
            pltpu.VMEM((HEADS, KEYS, lanes), F32),
            pltpu.VMEM((HEADS, KEYS, lanes), BF16),
            pltpu.VMEM((HEADS, KEYS, lanes), BF16),
            pltpu.VMEM((2, 2 * SPAN, D), BF16),
            side, side, side,
            pltpu.VMEM((HEADS, 2, SPAN, D), BF16),
            side, side, side,
            pltpu.VMEM((2, ROWS, width), BF16),
            pltpu.VMEM((HEADS, 2, SPAN, D), BF16),
            pltpu.VMEM((HEADS, HEADS, D), F32),
            pltpu.VMEM((HEADS, HEADS, D), F32),
            sem((HEADS, 2)), sem((HEADS, 2)), sem((HEADS, 2)), sem((HEADS, 2)),
            sem((2, 2)), sem((2, 2)), sem((HEADS, 2)), sem((HEADS, 2)),
            sem((HEADS, 2)), sem((HEADS, 2)), sem((HEADS, 2)), sem((HEADS, 2)),
            sem((2, 2)), sem((2, 2)), sem((HEADS, 2)), sem((HEADS, 2)),
            sem((HEADS,)), sem((HEADS,)), sem((13,)), sem((2, HEADS)),
        ],
        compiler_params=pltpu.CompilerParams(collective_id=0, has_side_effects=True, vmem_limit_bytes=VMEM_LIMIT),
    )(
        *[
            pltpu.with_memory_space_constraint(x, pltpu.HBM)
            for x in (span_order, doc_lengths.reshape(1, D), queries, dout, keys, values)
        ]
    )
    results = pl.pallas_call(
        write_kernel,
        out_shape=(tokens, tokens, grad, grad, entropy),
        in_specs=[whole] * 5,
        out_specs=(hbm, hbm, hbm, hbm, hbm),
        scratch_shapes=[sem((3 + 2 * HEADS,))],
        compiler_params=pltpu.CompilerParams(vmem_limit_bytes=8 << 20),
    )(*results)
    out, dq, dk, dv, ent = results
    return out, ent.T, dq, dk, dv


def solution(mesh):
    rows = P(("inner", "outer", "head"), None)
    return jax.shard_map(
        body,
        mesh=mesh,
        in_specs=(rows, rows, rows, rows, P(), P()),
        out_specs=(rows, P(("inner", "outer"), "head"), rows, rows, rows),
        check_vma=False,
    )
```

```python
import math

import jax
import jax.numpy as jnp
from jax import lax
from jax.experimental import pallas as pl
from jax.experimental.pallas import tpu as pltpu
from jax.sharding import PartitionSpec as P

MESH = pl.DeviceIdType.MESH
F32 = jnp.float32
BF16 = jnp.bfloat16
NEG = -1.0e30
LN2 = math.log(2.0)

D = 128
HEADS = 8
ROWS = 64
SPAN = 256
KEYS = 320
STEPS = SPAN // ROWS
PER = 4
SPLIT = 6
SPLIT_ROWS = 3
FAR = (4, 3, 5, 2, 6, 1, 7)
NEXT = (7, 6, 5, 4, 3, 2, 1)
VMEM_LIMIT = 40 << 20


def place():
    me = lax.axis_index("head")
    outer_size = lax.axis_size("outer")
    cycle = lax.axis_size("inner") * outer_size
    own = lax.axis_index("inner") * outer_size + lax.axis_index("outer")

    def at(index):
        return {"inner": index // outer_size, "outer": lax.rem(index, outer_size)}

    above = at(lax.rem(own + 1, cycle))
    below = at(lax.rem(own + cycle - 1, cycle))
    return me, me // STEPS, lax.rem(me, STEPS), own, cycle, above, below


def greet(me, above, below):
    barrier = pltpu.get_barrier_semaphore()
    for step in range(1, HEADS):
        pl.semaphore_signal(
            barrier, inc=1, device_id={"head": lax.rem(me + step, HEADS)}, device_id_type=MESH
        )
    pl.semaphore_signal(barrier, inc=1, device_id=above, device_id_type=MESH)
    pl.semaphore_signal(barrier, inc=1, device_id=below, device_id_type=MESH)
    return barrier


def remote(src, dst, send, recv, device):
    return pltpu.make_async_remote_copy(
        src_ref=src, dst_ref=dst, send_sem=send, recv_sem=recv, device_id=device, device_id_type=MESH
    )


def kernel(
    order_hbm, len_hbm, q_hbm, do_hbm, k_ref, v_ref,
    outs, dqs, dk_ref, dv_ref, ent_out,
    order_ref, len_ref, bias_ref, qs, dos, kk, vv, gk, gv, own_grad, pf, pb, dsb,
    hb, nb, rb, sel, cb, tnb, trb, tsel, xb, ob, es, eb,
    s1_send, s1_recv, own_send, own_recv, s2_send, s2_recv, s3_send, s3_recv,
    t1_send, t1_recv, town_send, town_recv, t2_send, t2_recv, t3_send, t3_recv,
    e_send, e_recv, local, q_sem,
):
    me, half, j, own, cycle, above, below = place()
    ins, keep, grads = (k_ref, v_ref), (kk, vv), (gk, gv)
    barrier = greet(me, above, below)
    width = HEADS * D
    loads = []
    facts = [
        pltpu.make_async_copy(order_hbm, order_ref, local.at[11]),
        pltpu.make_async_copy(len_hbm, len_ref, local.at[12]),
    ]
    for copy in facts:
        copy.start()
    for h in range(HEADS):
        cols = pl.ds(h * width, width)
        loads.append(pltpu.make_async_copy(q_hbm.at[:, cols], qs.at[h], q_sem.at[0, h]))
        loads.append(pltpu.make_async_copy(do_hbm.at[:, cols], dos.at[h], q_sem.at[1, h]))

    def each(action):
        for p in range(HEADS):
            @pl.when(me != p)
            def _(p=p):
                action(p)

    def around(order, action):
        for step in order:
            action(lax.rem(me + step, HEADS))

    def around_sized(order, action):
        for step in order:
            p = lax.rem(me + step, HEADS)
            for jj in range(STEPS):
                @pl.when(lax.rem(p, STEPS) == jj)
                def _(p=p, jj=jj):
                    action(p, jj)

    def branch(action):
        for jj in range(STEPS):
            @pl.when(j == jj)
            def _(jj=jj):
                action(jj)

    def later(action):
        for jj in range(1, STEPS):
            @pl.when(j == jj)
            def _(jj=jj):
                action(jj)

    def lanes_of(p):
        return pl.ds(p * D if isinstance(p, int) else pl.multiple_of(p * D, D), D)

    def spread(p, kv, src):
        return remote(
            ins[kv].at[:, lanes_of(p)], hb.at[kv, pl.ds(src * ROWS, ROWS)],
            s1_send.at[p, kv], s1_recv.at[src, kv], {"head": p},
        )

    def share(p, kv, src, jj):
        return remote(
            hb.at[kv, pl.ds((p // STEPS) * SPAN, jj * ROWS)],
            keep[kv].at[pl.ds(SPAN, jj * ROWS), pl.ds(src * D, D)],
            own_send.at[p, kv], own_recv.at[src, kv], {"head": p},
        )

    def share_mine(kv, jj):
        return pltpu.make_async_copy(
            hb.at[kv, pl.ds(half * SPAN, jj * ROWS)],
            keep[kv].at[pl.ds(SPAN, jj * ROWS), pl.ds(me * D, D)], local.at[7 + kv],
        )

    def pass_on(side, kv):
        return remote(
            nb.at[side, kv], rb.at[side, kv], s2_send.at[side, kv], s2_recv.at[side, kv],
            (above, below)[side],
        )

    def deliver(p, kv, src, jj):
        rows = pl.ds(jj * ROWS, SPAN - jj * ROWS)
        return remote(
            sel.at[p // STEPS, kv, rows], keep[kv].at[rows, pl.ds(src * D, D)],
            s3_send.at[p, kv], s3_recv.at[src, kv], {"head": p},
        )

    def collect(p, kv, src, jj):
        rows = pl.ds(jj * ROWS, SPAN - jj * ROWS)
        return remote(
            grads[kv].at[rows, pl.ds(p * D, D)], cb.at[src, kv, rows],
            t3_send.at[p, kv], t3_recv.at[src, kv], {"head": p},
        )

    def share_back(p, kv, src, jj):
        return remote(
            grads[kv].at[pl.ds(SPAN, jj * ROWS), pl.ds(p * D, D)],
            ob.at[src, kv, pl.ds(0, jj * ROWS)],
            town_send.at[p, kv], town_recv.at[src, kv], {"head": p},
        )

    def share_back_mine(kv, jj):
        return pltpu.make_async_copy(
            grads[kv].at[pl.ds(SPAN, jj * ROWS), pl.ds(me * D, D)],
            ob.at[me, kv, pl.ds(0, jj * ROWS)], local.at[9 + kv],
        )

    def pass_back(side, kv):
        return remote(
            tnb.at[side, kv], trb.at[side, kv], t2_send.at[side, kv], t2_recv.at[side, kv],
            (below, above)[side],
        )

    def give_back(p, kv, src):
        return remote(
            tsel.at[p // STEPS, kv, pl.ds(lax.rem(p, STEPS) * ROWS, ROWS)],
            xb.at[kv, :, pl.ds(src * D, D)],
            t1_send.at[p, kv], t1_recv.at[src, kv], {"head": p},
        )

    def entropy_to(p, src):
        return remote(es.at[p], eb.at[src], e_send.at[p], e_recv.at[src], {"head": p})

    pl.semaphore_wait(barrier, HEADS + 1)
    for kv in range(2):
        around(FAR, lambda p: spread(p, kv, me).start())
    mine = [
        pltpu.make_async_copy(
            ins[kv].at[:, pl.ds(me * D, D)], hb.at[kv, pl.ds(me * ROWS, ROWS)], local.at[kv]
        )
        for kv in range(2)
    ] + [
        pltpu.make_async_copy(
            ins[kv], keep[kv].at[pl.ds(SPAN + j * ROWS, ROWS)], local.at[2 + kv]
        )
        for kv in range(2)
    ]
    for copy in mine + loads:
        copy.start()

    for copy in facts:
        copy.wait()
    first_low = order_ref[2 * own] == own
    start_pos = order_ref[2 * own + half] * SPAN + j * ROWS
    lens = jnp.broadcast_to(len_ref[...], (D, D)).astype(F32)
    row = lax.broadcasted_iota(jnp.int32, (D, D), 0)
    col = lax.broadcasted_iota(jnp.int32, (D, D), 1)
    starts = jnp.sum(jnp.where(col < row, lens, 0.0), axis=1, keepdims=True)
    pos = (start_pos + lax.rem(col, ROWS)).astype(F32)
    found = jnp.max(jnp.where(starts <= pos, starts, 0.0), axis=0, keepdims=True)
    first = found - (start_pos - SPAN).astype(F32)
    key = lax.broadcasted_iota(jnp.int32, (KEYS, D), 0)
    query = lax.rem(lax.broadcasted_iota(jnp.int32, (KEYS, D), 1), ROWS)
    allowed = (key.astype(F32) >= first) & (key <= query + SPAN)
    bias_ref[...] = jnp.where(allowed, 0.0, NEG)
    for copy in mine:
        copy.wait()

    for kv in range(2):
        each(lambda p: spread(p, kv, p).wait_recv())
        a, b = hb[kv, :SPAN], hb[kv, SPAN:]
        nb[0, kv] = jnp.where(first_low, a, b)
        nb[1, kv] = jnp.where(first_low, b, a)
        pass_on(0, kv).start()
        pass_on(1, kv).start()
    for kv in range(2):
        later(lambda jj: share_mine(kv, jj).start())
        each(lambda p: share(p, kv, me, p % STEPS).start() if p % STEPS else None)
    back = []
    for kv in range(2):
        pass_on(0, kv).wait_recv()
        pass_on(1, kv).wait_recv()
        prev_low = rb[0, kv]
        prev_high = jnp.where(own == cycle - 1, nb[0, kv], rb[1, kv])
        sel[0, kv] = jnp.where(first_low, prev_low, prev_high)
        sel[1, kv] = jnp.where(first_low, prev_high, prev_low)
        each(lambda p: deliver(p, kv, me, p % STEPS).start())
        copy = pltpu.make_async_copy(
            sel.at[half, kv], keep[kv].at[pl.ds(0, SPAN), pl.ds(me * D, D)], local.at[kv]
        )
        copy.start()
        back.append(copy)

    scale = 1.0 / math.sqrt(D)
    nt = (((1,), (1,)), ((), ()))
    nn = (((1,), (0,)), ((), ()))
    lanes = PER * ROWS
    rows = pl.multiple_of(j * ROWS, ROWS)
    window = pl.ds(rows, KEYS)
    sub = lax.broadcasted_iota(jnp.int32, (HEADS, D), 0)

    def columns(h):
        return pl.ds(pl.multiple_of(h * D, D), D)

    def stacked(ref, h, chunk):
        return jnp.concatenate(
            [ref[h, :, g * D : (g + 1) * D] for g in range(chunk * PER, (chunk + 1) * PER)], axis=0
        )

    def arrive(step, h, kv):
        @pl.when(step > 0)
        def _():
            branch(lambda jj: deliver(h, kv, h, jj).wait_recv())
            later(lambda jj: share(h, kv, h, jj).wait_recv())

    def leave(step, h, kv):
        @pl.when(step > 0)
        def _():
            branch(lambda jj: collect(h, kv, me, jj).start())

    def store_grad(kv, h, total):
        grads[kv][pl.ds(rows, SPAN), columns(h)] = total[:SPAN].astype(BF16)
        own_grad[kv, :, columns(h)] = total[SPAN:]

    def score_step(step, carry):
        h = lax.rem(me + step, HEADS)
        arrive(step, h, 0)
        k5 = kk[window, columns(h)]
        bias = jnp.concatenate([bias_ref[...]] * (lanes // D), axis=1)
        ent = jnp.zeros((HEADS, D), F32)
        dv = jnp.zeros((KEYS, D), F32)
        for chunk in range(HEADS // PER):
            at = slice(chunk * lanes, (chunk + 1) * lanes)
            q, do = stacked(qs, h, chunk), stacked(dos, h, chunk)
            t = lax.dot_general(k5, q, nt, preferred_element_type=F32) * (scale / LN2) + bias
            u = t - jnp.max(t, axis=0, keepdims=True)
            e = jnp.exp2(u)
            total = jnp.sum(e, axis=0, keepdims=True)
            p = e * (1.0 / total)
            spread_sum = jnp.sum(p * u, axis=0, keepdims=True)
            entropy = LN2 * (jnp.log2(total) - spread_sum)
            pf[h, :, at] = p
            rounded = p.astype(BF16)
            pb[h, :, at] = rounded
            dv = dv + lax.dot_general(rounded, do, nn, preferred_element_type=F32)
            for n in range(PER // 2):
                pair = jnp.broadcast_to(entropy[:, n * D : (n + 1) * D], (HEADS, D))
                g = chunk * PER + 2 * n
                ent = jnp.where(sub == g, pair, ent)
                ent = jnp.where(sub == g + 1, pltpu.roll(pair, ROWS, 1), ent)
        es[h] = ent
        store_grad(1, h, dv)
        leave(step, h, 1)

        @pl.when(step > 0)
        def _():
            entropy_to(h, me).start()

        return carry

    def slope_step(step, carry):
        h = lax.rem(me + step, HEADS)
        arrive(step, h, 1)
        v5 = vv[window, columns(h)]
        dk = jnp.zeros((KEYS, D), F32)
        for chunk in range(HEADS // PER):
            at = slice(chunk * lanes, (chunk + 1) * lanes)
            q, do = stacked(qs, h, chunk), stacked(dos, h, chunk)
            dp = lax.dot_general(v5, do, nt, preferred_element_type=F32)
            p = pf[h, :, at]
            delta = jnp.sum(p * dp, axis=0, keepdims=True)
            ds = (p * ((dp - delta) * scale)).astype(BF16)
            dsb[h, :, at] = ds
            dk = dk + lax.dot_general(ds, q, nn, preferred_element_type=F32)
        store_grad(0, h, dk)
        leave(step, h, 0)
        return carry

    def row_step(h, carry):
        k5t, v5t = kk[window, columns(h)].T, vv[window, columns(h)].T
        for chunk in range(HEADS // PER):
            at = slice(chunk * lanes, (chunk + 1) * lanes)
            out = lax.dot_general(v5t, pb[h, :, at], nn, preferred_element_type=F32).T
            dq = lax.dot_general(k5t, dsb[h, :, at], nn, preferred_element_type=F32).T
            for n in range(PER):
                g = chunk * PER + n
                outs[h, :, g * D : (g + 1) * D] = out[n * ROWS : (n + 1) * ROWS].astype(BF16)
                dqs[h, :, g * D : (g + 1) * D] = dq[n * ROWS : (n + 1) * ROWS].astype(BF16)
        return carry

    def summed(kv):
        sides = []
        for side in range(2):
            blocks = []
            for b in range(STEPS):
                at = slice(b * ROWS, (b + 1) * ROWS)
                total = cb[side * STEPS, kv, at].astype(F32)
                for jj in range(1, b + 1):
                    total = total + cb[side * STEPS + jj, kv, at].astype(F32)
                blocks.append(total.astype(BF16))
            sides.append(jnp.concatenate(blocks, axis=0))
        tnb[0, kv] = jnp.where(first_low, sides[0], sides[1])
        tnb[1, kv] = jnp.where(first_low, sides[1], sides[0])

    def keep_mine(kv):
        return pltpu.make_async_copy(
            grads[kv].at[pl.ds(0, SPAN), pl.ds(me * D, D)], cb.at[me, kv], local.at[5 + kv]
        )

    def send_sums(kv):
        each(lambda p: collect(p, kv, p, p % STEPS).wait_recv())
        keep_mine(kv).wait()
        summed(kv)
        pass_back(0, kv).start()
        pass_back(1, kv).start()

    def send_shares(kv):
        later(lambda jj: share_back_mine(kv, jj).start())
        later(lambda jj: each(lambda p: share_back(p, kv, me, jj).start()))

    def own_sum(kv, side):
        blocks = []
        for b in range(STEPS):
            at = slice(b * ROWS, (b + 1) * ROWS)
            total = jnp.zeros((ROWS, D), F32)
            for jj in range(b + 1, STEPS):
                total = total + ob[side * STEPS + jj, kv, at].astype(F32)
            blocks.append(total)
        return jnp.concatenate(blocks, axis=0)

    def keep_given(kv):
        return pltpu.make_async_copy(
            tsel.at[half, kv, pl.ds(j * ROWS, ROWS)], xb.at[kv, :, pl.ds(me * D, D)],
            local.at[2 + kv],
        )

    def send_given(kv):
        each(lambda p: share_back(p, kv, p, p % STEPS).wait_recv() if p % STEPS else None)
        later(lambda jj: share_back_mine(kv, jj).wait())
        pass_back(0, kv).wait_recv()
        pass_back(1, kv).wait_recv()
        low_part = jnp.where(own == cycle - 1, tnb[1, kv], trb[0, kv]).astype(F32)
        high_part = jnp.where(own == 0, jnp.zeros_like(trb[1, kv]), trb[1, kv]).astype(F32)
        first_part = jnp.where(first_low, low_part, high_part) + own_sum(kv, 0)
        second_part = jnp.where(first_low, high_part, low_part) + own_sum(kv, 1)
        tsel[0, kv] = first_part.astype(BF16)
        tsel[1, kv] = second_part.astype(BF16)
        each(lambda p: give_back(p, kv, me).start())
        keep_given(kv).start()

    def finish(kv, dst):
        keep_given(kv).wait()
        each(lambda p: give_back(p, kv, p).wait_recv())
        dst[...] = (own_grad[kv] + xb[kv].astype(F32)).astype(BF16)

    for copy in loads:
        copy.wait()
    back[0].wait()
    later(lambda jj: share_mine(0, jj).wait())
    lax.fori_loop(0, HEADS, score_step, 0)
    keep_mine(1).start()
    send_shares(1)
    back[1].wait()
    later(lambda jj: share_mine(1, jj).wait())
    lax.fori_loop(0, SPLIT, slope_step, 0)
    send_sums(1)
    lax.fori_loop(SPLIT, HEADS, slope_step, 0)
    keep_mine(0).start()
    send_shares(0)
    lax.fori_loop(0, SPLIT_ROWS, row_step, 0)
    send_sums(0)
    send_given(1)
    lax.fori_loop(SPLIT_ROWS, HEADS, row_step, 0)
    send_given(0)
    finish(1, dv_ref)
    local_ent = pltpu.make_async_copy(es.at[me], eb.at[me], local.at[4])
    local_ent.start()
    local_ent.wait()
    each(lambda p: entropy_to(p, p).wait_recv())
    for n in range(HEADS // 2):
        ent_out[:, n * D : n * D + ROWS] = eb[2 * n, :, :ROWS]
        ent_out[:, n * D + ROWS : (n + 1) * D] = eb[2 * n + 1, :, :ROWS]
    finish(0, dk_ref)
    for kv in range(2):
        branch(lambda jj: each(lambda p: collect(p, kv, me, jj).wait_send()))

        def sent(p):
            spread(p, kv, me).wait_send()
            deliver(p, kv, me, p % STEPS).wait_send()
            give_back(p, kv, me).wait_send()
            if p % STEPS:
                share(p, kv, me, p % STEPS).wait_send()

        each(sent)
        later(lambda jj: each(lambda p: share_back(p, kv, me, jj).wait_send()))
        for side in range(2):
            pass_on(side, kv).wait_send()
            pass_back(side, kv).wait_send()
    each(lambda p: entropy_to(p, me).wait_send())


def write_kernel(outs, dqs, dk, dv, ent, out_hbm, dq_hbm, dk_hbm, dv_hbm, ent_hbm, sems):
    width = HEADS * D
    copies = [
        pltpu.make_async_copy(src, dst, sems.at[n])
        for n, (src, dst) in enumerate(((dk, dk_hbm), (dv, dv_hbm), (ent, ent_hbm)))
    ]
    for h in range(HEADS):
        cols = pl.ds(h * width, width)
        copies.append(pltpu.make_async_copy(outs.at[h], out_hbm.at[:, cols], sems.at[3 + 2 * h]))
        copies.append(pltpu.make_async_copy(dqs.at[h], dq_hbm.at[:, cols], sems.at[4 + 2 * h]))
    for copy in copies:
        copy.start()
    for copy in copies:
        copy.wait()


def body(queries, keys, values, dout, doc_lengths, span_order):
    sem = pltpu.SemaphoreType.DMA
    hbm = pl.BlockSpec(memory_space=pl.ANY)
    whole = pl.BlockSpec(memory_space=pltpu.VMEM)
    width = HEADS * D
    lanes = HEADS * ROWS
    stacked = jax.ShapeDtypeStruct((HEADS, ROWS, width), BF16)
    tokens = jax.ShapeDtypeStruct((ROWS, HEADS * width), BF16)
    grad = jax.ShapeDtypeStruct((ROWS, width), BF16)
    entropy = jax.ShapeDtypeStruct((HEADS, 2 * SPAN), F32)
    side = pltpu.VMEM((2, 2, SPAN, D), BF16)
    results = pl.pallas_call(
        kernel,
        out_shape=(stacked, stacked, grad, grad, entropy),
        in_specs=[pl.BlockSpec(memory_space=pltpu.HBM)] * 6,
        out_specs=(whole, whole, whole, whole, whole),
        scratch_shapes=[
            pltpu.SMEM((span_order.shape[0],), jnp.int32),
            pltpu.VMEM((1, D), jnp.int32),
            pltpu.VMEM((KEYS, D), F32),
            pltpu.VMEM((HEADS, ROWS, width), BF16),
            pltpu.VMEM((HEADS, ROWS, width), BF16),
            pltpu.VMEM((2 * SPAN, width), BF16),
            pltpu.VMEM((2 * SPAN, width), BF16),
            pltpu.VMEM((2 * SPAN, width), BF16),
            pltpu.VMEM((2 * SPAN, width), BF16),
            pltpu.VMEM((2, ROWS, width), F32),
            pltpu.VMEM((HEADS, KEYS, lanes), F32),
            pltpu.VMEM((HEADS, KEYS, lanes), BF16),
            pltpu.VMEM((HEADS, KEYS, lanes), BF16),
            pltpu.VMEM((2, 2 * SPAN, D), BF16),
            side, side, side,
            pltpu.VMEM((HEADS, 2, SPAN, D), BF16),
            side, side, side,
            pltpu.VMEM((2, ROWS, width), BF16),
            pltpu.VMEM((HEADS, 2, SPAN, D), BF16),
            pltpu.VMEM((HEADS, HEADS, D), F32),
            pltpu.VMEM((HEADS, HEADS, D), F32),
            sem((HEADS, 2)), sem((HEADS, 2)), sem((HEADS, 2)), sem((HEADS, 2)),
            sem((2, 2)), sem((2, 2)), sem((HEADS, 2)), sem((HEADS, 2)),
            sem((HEADS, 2)), sem((HEADS, 2)), sem((HEADS, 2)), sem((HEADS, 2)),
            sem((2, 2)), sem((2, 2)), sem((HEADS, 2)), sem((HEADS, 2)),
            sem((HEADS,)), sem((HEADS,)), sem((13,)), sem((2, HEADS)),
        ],
        compiler_params=pltpu.CompilerParams(collective_id=0, has_side_effects=True, vmem_limit_bytes=VMEM_LIMIT),
    )(
        *[
            pltpu.with_memory_space_constraint(x, pltpu.HBM)
            for x in (span_order, doc_lengths.reshape(1, D), queries, dout, keys, values)
        ]
    )
    results = pl.pallas_call(
        write_kernel,
        out_shape=(tokens, tokens, grad, grad, entropy),
        in_specs=[whole] * 5,
        out_specs=(hbm, hbm, hbm, hbm, hbm),
        scratch_shapes=[sem((3 + 2 * HEADS,))],
        compiler_params=pltpu.CompilerParams(vmem_limit_bytes=8 << 20),
    )(*results)
    out, dq, dk, dv, ent = results
    return out, ent.T, dq, dk, dv


def solution(mesh):
    rows = P(("inner", "outer", "head"), None)
    return jax.shard_map(
        body,
        mesh=mesh,
        in_specs=(rows, rows, rows, rows, P(), P()),
        out_specs=(rows, P(("inner", "outer"), "head"), rows, rows, rows),
        check_vma=False,
    )
```
